512 devices in a mesh: dom: 32 (over x, y_hi, core), bucket: 8 (over z), depth: 2 (over y_lo).
Axes of the slice: x: 4, y: 8 (y_hi: 4, y_lo: 2; y = y_hi * 2 + y_lo), z: 8, core: 2. Of those that a mesh axis runs over, the one named last changes fastest.
Arguments:
- entities: float32 [262144, 400], P(('dom', 'bucket')), may hold values from -7 to 7
- entity_state: float32 [262144], P(('dom', 'bucket')), may hold values from 0.05 to 0.5
- relations: float32 [256, 400], replicated, may hold values from 0.5 to 2
- relation_state: float32 [256], replicated, may hold values from 0.05 to 0.5
- edge_ends: int32 [2, 262144], P(None, ('dom', 'bucket')), may hold values from 0 to 1023
- relation_ids: int32 [262144], P(('dom', 'bucket')), may hold values from 0 to 255
- neg_ids: int32 [512, 1024], P(('dom', 'bucket'), 'depth'), may hold values from 0 to 1023
- edge_count: int32 [256], P(('dom', 'bucket')), may hold values from 16 to 1024, as said below
Outputs:
- new_entities: float32 [262144, 400], P(('dom', 'bucket'))
- new_state: float32 [262144], P(('dom', 'bucket'))
- new_relations: float32 [256, 400], replicated
The draws below stay inside these ranges and needn't reach their ends.
Inputs may be any that keep to these rules, and one draw needn't show every extreme that they name: `edge_count`: the live slots of a partition are its first ones; partition 0 is full in every draw.
All inputs are finite; a program needn't handle non-finite values.
Results may differ from the reference program's by a relative error of at most 0.0006.
The reference program's roundings to bfloat16 on the way count: a program that leaves them out, or rounds other values in their place, can miss the bound.
Values may be sent and summed in bfloat16 or wider, within the bound.
No kernel may reach another device: no remote copies, remote signals or barrier semaphores. Data moves between devices by JAX's collectives and lax.ppermute only.
A program may use at most 64 MiB of HBM per device.

```python
import math
import jax
import jax.numpy as jnp
import numpy as np
from jax import lax

D = 400
NREL = 256
ENT_DEV = 1024
BLOCK = 512
BLOCKS = 2
NEG = 1024
PARTS_SIZE = 256
EDGE_DEV = 1024
ENT = 262144
EDGES = 262144
N_DOM = 32
N_BUCKET = 8


def draw_entities(key, part):
    key_row, key_value, key_dir, key_level = jax.random.split(jax.random.fold_in(key, 11), 4)
    row_scale = jnp.exp(jax.random.uniform(key_row, (ENT, 1), minval=math.log(0.12), maxval=math.log(1.2)))
    values = jax.random.normal(key_value, (ENT, D)) * row_scale
    signs = jnp.where(jax.random.normal(key_dir, (1, D)) >= 0.0, 1.0, -1.0)
    amplitude = jnp.sqrt(182.0 / D)
    level = jax.random.uniform(key_level, (ENT, 1), minval=0.8, maxval=1.2)
    slot_index = jnp.arange(ENT, dtype=jnp.int32) % ENT_DEV
    aligned = slot_index < ENT_DEV // 4
    values = jnp.where(aligned[:, None], signs * amplitude * level + 0.1 * values, values)
    return jnp.clip(values, -7.0, 7.0).astype(jnp.float32)


def draw_edge_count(key, part):
    key_base, key_shift = jax.random.split(jax.random.fold_in(key, 5))
    base_count = jax.random.randint(key_base, (PARTS_SIZE,), EDGE_DEV // 8, EDGE_DEV + 1)
    shift_count = jax.random.randint(key_shift, (PARTS_SIZE,), 0, 4)
    counts = jnp.right_shift(base_count, shift_count)
    counts = counts.at[0].set(EDGE_DEV)
    return counts.astype(jnp.int32)


def plant(entries, stream_key, least, high):
    longest = entries.shape.index(max(entries.shape))
    spots = []
    for shift in (0, 1):
        where = [jax.random.randint(jax.random.fold_in(stream_key, axis), (), 0, length) for axis, length in enumerate(entries.shape)]
        where[longest] = (where[longest] + shift) % entries.shape[longest]
        spots.append(tuple(where))
    return entries.at[spots[0]].set(least).at[spots[1]].set(high)


def level_of(key, shape, shards, smallest, high):
    loudness = 1.0
    for axis_at, blocks in shards:
        draws = jax.random.uniform(jax.random.fold_in(jax.random.fold_in(key, 6), axis_at), (blocks,), jnp.float32, smallest / len(shards), high / len(shards))
        loudness = loudness * jnp.repeat(jnp.exp(draws), shape[axis_at] // blocks).reshape((-1,) + (1,) * (len(shape) - 1 - axis_at))
    return loudness


def rank_bounds(number_of, skew):
    loads = [(1 << 20) // math.isqrt(grade ** skew) + 1 for grade in range(1, number_of + 1)]
    width = 1 + sum(loads) // (1 << 30)
    return np.cumsum(np.array([max(1, weight // width) for weight in loads]))


def ranked(rng, dims, amount, skew):
    table = rank_bounds(amount, skew)
    ticket = jax.random.randint(jax.random.fold_in(rng, 1), dims, 0, int(table[amount - 1]))
    grade = jnp.searchsorted(jnp.asarray(table, jnp.int32), ticket, side="right")
    return jax.random.permutation(jax.random.fold_in(rng, 2), amount)[grade].astype(jnp.int32)


def setup_inputs(seed: int = 0) -> dict:
    keys = jax.random.split(jax.random.key(seed), 9)
    entities = draw_entities(jax.random.fold_in(keys[8], 71), 0)
    entity_state = jnp.clip(jnp.exp(math.log(0.5) - 2.3025851 * jax.random.uniform(keys[1], (ENT,), jnp.float32) ** level_of(keys[1], (ENT,), ((0, 256),), -0.2, 0.2)), 0.05, 0.5)
    relations = jnp.clip(jnp.exp(jax.random.uniform(keys[2], (NREL, D), jnp.float32, math.log(0.5), math.log(2.0))), 0.5, 2.0)
    relation_state = jnp.clip(jnp.exp(jax.random.uniform(keys[3], (NREL,), jnp.float32, math.log(0.05), math.log(0.5))), 0.05, 0.5)
    edge_ends = plant(jax.random.randint(keys[4], (2, EDGES), 0, ENT_DEV), jax.random.fold_in(keys[4], 1), 0, ENT_DEV - 1).astype(jnp.int32)
    relation_ids = plant(ranked(keys[5], (EDGES,), NREL, 3), jax.random.fold_in(keys[5], 3), 0, NREL - 1).astype(jnp.int32)
    neg_ids = plant(jax.random.randint(keys[6], (PARTS_SIZE * BLOCKS, NEG), 0, ENT_DEV), jax.random.fold_in(keys[6], 1), 0, ENT_DEV - 1).astype(jnp.int32)
    edge_count = draw_edge_count(jax.random.fold_in(keys[8], 71), 0)
    return dict(entities=entities, entity_state=entity_state, relations=relations, relation_state=relation_state, edge_ends=edge_ends, relation_ids=relation_ids, neg_ids=neg_ids, edge_count=edge_count)


entity_rate = 0.1
relation_rate = 1.0

def block_grads(own_rows, far_rows, relations, left_ids, right_ids, rel_ids, active, negative_ids):
    left_rows = own_rows[left_ids]
    right_rows = far_rows[right_ids]
    scaling = relations[rel_ids]
    queries = (left_rows.astype(jnp.float32) * scaling).astype(jnp.bfloat16)
    negatives = far_rows[negative_ids]
    positive = lax.optimization_barrier(jnp.sum(queries.astype(jnp.float32) * right_rows.astype(jnp.float32), axis=1))
    scores = lax.dot_general(queries, negatives, (((1,), (1,)), ((), ())), preferred_element_type=jnp.float32)
    peak = jnp.maximum(positive, lax.optimization_barrier(jnp.max(scores, axis=1)))
    shifted = jnp.exp(scores - peak[:, None])
    denom = jnp.exp(positive - peak) + lax.optimization_barrier(jnp.sum(shifted, axis=1))
    weights = (shifted * (active / denom)[:, None]).astype(jnp.bfloat16)
    pos_coef = active * (jnp.exp(positive - peak) / denom - 1.0)
    query_grad = jnp.dot(weights, negatives, preferred_element_type=jnp.float32) + pos_coef[:, None] * right_rows.astype(jnp.float32)
    left_grad = query_grad * scaling
    rel_term = query_grad * left_rows.astype(jnp.float32)
    right_grad = pos_coef[:, None] * queries.astype(jnp.float32)
    neg_grad = lax.dot_general(weights, queries, (((0,), (0,)), ((), ())), preferred_element_type=jnp.float32)
    return (left_grad, rel_term, right_grad, neg_grad)

def partition_grads(own_rows, far_rows, relations, edge_rows, rel_row, neg_table, live_count):
    offsets = jnp.arange(BLOCK, dtype=jnp.int32)

    def block_step(totals_in, block_index):
        own_grad, far_grad, rel_grad = totals_in
        first_slot = (block_index * BLOCK).astype(jnp.int32)
        left_ids = lax.dynamic_slice_in_dim(edge_rows[0], first_slot, BLOCK)
        right_ids = lax.dynamic_slice_in_dim(edge_rows[1], first_slot, BLOCK)
        rel_ids = lax.dynamic_slice_in_dim(rel_row, first_slot, BLOCK)
        negative_ids = lax.dynamic_index_in_dim(neg_table, block_index, 0, keepdims=False)
        active = (first_slot + offsets < live_count).astype(jnp.float32)
        left_grad, rel_term, right_grad, neg_grad = block_grads(own_rows, far_rows, relations, left_ids, right_ids, rel_ids, active, negative_ids)
        own_grad = own_grad.at[left_ids].add(left_grad)
        far_grad = far_grad.at[right_ids].add(right_grad).at[negative_ids].add(neg_grad)
        rel_grad = rel_grad.at[rel_ids].add(rel_term)
        return ((own_grad, far_grad, rel_grad), None)
    zeros_rows = jnp.zeros((ENT_DEV, D), jnp.float32)
    start_totals = (zeros_rows, zeros_rows, jnp.zeros((NREL, D), jnp.float32))
    result, unused = lax.scan(block_step, start_totals, jnp.arange(BLOCKS, dtype=jnp.int32))
    return result

def reference(entities, entity_state, relations, relation_state, edge_ends, relation_ids, neg_ids, edge_count):
    part_count = N_DOM * N_BUCKET
    own_grid = entities.astype(jnp.bfloat16).reshape(N_DOM, N_BUCKET, ENT_DEV, D)
    far_all = jnp.roll(own_grid, N_DOM // 2, axis=0).reshape(part_count, ENT_DEV, D)
    own_all = own_grid.reshape(part_count, ENT_DEV, D)
    edge_table = edge_ends.reshape(2, part_count, EDGE_DEV).transpose(1, 0, 2)
    rel_table = relation_ids.reshape(part_count, EDGE_DEV)
    neg_tables = neg_ids.reshape(part_count, BLOCKS, NEG)

    def visit_part(rel_total, visit_item):
        own_rows, far_rows, edge_rows, rel_row, neg_table, live_count = visit_item
        own_grad, far_grad, rel_grad = partition_grads(own_rows, far_rows, relations, edge_rows, rel_row, neg_table, live_count)
        return (rel_total + rel_grad, (own_grad, far_grad))
    rel_total, grads = lax.scan(visit_part, jnp.zeros((NREL, D), jnp.float32), (own_all, far_all, edge_table, rel_table, neg_tables, edge_count))
    own_grads, far_grads = grads
    far_home = jnp.roll(far_grads.reshape(N_DOM, N_BUCKET, ENT_DEV, D), N_DOM // 2, axis=0).reshape(ENT, D)
    entity_grad = own_grads.reshape(ENT, D) + far_home
    new_state = entity_state + lax.optimization_barrier(jnp.mean(entity_grad * entity_grad, axis=1))
    new_entities = entities - entity_rate * entity_grad / jnp.sqrt(new_state)[:, None]
    rel_state = relation_state + lax.optimization_barrier(jnp.mean(rel_total * rel_total, axis=1))
    new_relations = relations - relation_rate * rel_total / jnp.sqrt(rel_state)[:, None]
    return (new_entities, new_state, new_relations)
```

```python
import jax
import jax.numpy as jnp
from jax import lax
from jax.experimental import pallas as pl
from jax.experimental.pallas import tpu as pltpu
from jax.sharding import PartitionSpec as P

BLOCK = 512

entity_rate = 0.1
relation_rate = 1.0

F32 = jnp.float32
BF16 = jnp.bfloat16
NN = (((1,), (0,)), ((), ()))
NT = (((1,), (1,)), ((), ()))


def mm(a, b, dims=NN):
    return lax.dot_general(a, b, dims, preferred_element_type=F32)


def onehot(ids, rows):
    index = lax.broadcasted_iota(jnp.int32, (rows, ids.shape[1]), 0)
    return jnp.where(index == ids, 1.0, 0.0).astype(BF16)


def split(value, parts):
    out = []
    for _ in range(parts):
        piece = value.astype(BF16)
        out.append(piece)
        value = value - piece.astype(F32)
    return out


def prepare(own, rel, ends, rid, neg_a, neg_b, q, left, scale, count):
    rel_parts = split(rel[...], 3)
    ones = jnp.ones((neg_a.shape[1], 128), BF16)
    for c in range(q.shape[1] // BLOCK):
        lanes = slice(c * BLOCK, (c + 1) * BLOCK)
        picked = mm(own[...], onehot(ends[0:1, lanes], own.shape[1]))
        by_rel = onehot(rid[0:1, lanes], rel.shape[1])
        factor = sum(mm(part, by_rel) for part in rel_parts)
        q[:, lanes] = (picked * factor).astype(BF16)
        left[:, lanes] = picked.astype(BF16)
        scale[:, lanes] = factor
        hits = mm(onehot(neg_a[c : c + 1, :], own.shape[1]), ones)
        count[c] = hits + mm(onehot(neg_b[c : c + 1, :], own.shape[1]), ones)


CHUNK = 256


def block_lanes(block):
    return pl.ds(pl.multiple_of(block * BLOCK, BLOCK), BLOCK)


def softmax_coef(scores, times, right_ids, first, live):
    right = lax.broadcasted_iota(jnp.int32, scores.shape, 0) == right_ids
    positive = jnp.sum(jnp.where(right, scores, 0.0), axis=0, keepdims=True)
    masked = jnp.where(times > 0.0, scores, -3.0e38)
    peak = jnp.maximum(positive, jnp.max(masked, axis=0, keepdims=True))
    shifted = jnp.exp(masked - peak)
    top = jnp.exp(positive - peak)
    denom = top + jnp.sum(shifted * times, axis=0, keepdims=True)
    slot = lax.broadcasted_iota(jnp.int32, right_ids.shape, 1) + first
    active = jnp.where(slot < live, 1.0, 0.0)
    pos_coef = active * (top / denom - 1.0)
    weights = (shifted * (active / denom)).astype(BF16).astype(F32) * times
    return split(weights + jnp.where(right, pos_coef, 0.0), 2)


def own_block(
    block, live, ends, rid, far, q_hbm, left_hbm, scale_hbm, count_hbm,
    high_hbm, low_hbm, grad_hbm, rel_grad,
    q, left, scale, count, high, low, grad, sems,
):
    lanes = block_lanes(block[0])
    reads = [
        pltpu.make_async_copy(src, dst, sems.at[i])
        for i, (src, dst) in enumerate(
            [
                (q_hbm.at[:, lanes], q),
                (count_hbm.at[block[0]], count),
                (scale_hbm.at[:, lanes], scale),
                (left_hbm.at[:, lanes], left),
            ]
        )
    ]
    for read in reads:
        read.start()
    far_rows = far[...].T
    for read in reads[:2]:
        read.wait()
    times = jnp.tile(count[...], (1, CHUNK // 128))
    total, writes = None, []
    for c in range(BLOCK // CHUNK):
        part = slice(c * CHUNK, (c + 1) * CHUNK)
        first = pl.multiple_of(block[0] * BLOCK + c * CHUNK, CHUNK)
        ids = pl.ds(first, CHUNK)
        scores = mm(far_rows, q[:, part])
        upper, lower = softmax_coef(scores, times, ends[1:2, ids], first, live[0])
        high[:, part] = upper
        low[:, part] = lower
        query_grad = mm(far[...], upper) + mm(far[...], lower)
        if c == 0:
            for read in reads[2:]:
                read.wait()
        grad[:, part] = (query_grad * scale[:, part]).astype(BF16)
        for i, (src, dst) in enumerate([(high, high_hbm), (low, low_hbm), (grad, grad_hbm)]):
            write = pltpu.make_async_copy(
                src.at[:, part], dst.at[:, part], sems.at[4 + 3 * c + i]
            )
            write.start()
            writes.append(write)
        pieces = split(query_grad * left[:, part].astype(F32), 2)
        by_rel = onehot(rid[0:1, ids], rel_grad.shape[0])
        share = mm(by_rel, pieces[0], NT) + mm(by_rel, pieces[1], NT)
        total = share if total is None else total + share
    rel_grad[...] = total
    for write in writes:
        write.wait()


def dithered(value):
    row = lax.broadcasted_iota(jnp.int32, (value.shape[0], 1), 0).astype(F32) * 0.61803398875
    shift = (row - jnp.floor(row) - 0.5) * (1.0 / 256.0)
    return (value + value * shift).astype(BF16)


def other_block(
    block, live, ends, far_hbm, q_hbm, scale_hbm, count_hbm, high_hbm, low_hbm,
    far_grad, grad,
    far, q, scale, count, high, low, sems,
):
    lanes = block_lanes(1 - block[0])
    done = block_lanes(block[0])
    reads = [
        pltpu.make_async_copy(src, dst, sems.at[i])
        for i, (src, dst) in enumerate(
            [
                (far_hbm, far),
                (q_hbm, q),
                (count_hbm.at[1 - block[0]], count),
                (scale_hbm.at[:, lanes], scale),
                (high_hbm, high.at[:, done]),
                (low_hbm, low.at[:, done]),
            ]
        )
    ]
    for read in reads:
        read.start()
    for read in reads[:4]:
        read.wait()
    far_rows = far[...].T
    times = jnp.tile(count[...], (1, CHUNK // 128))
    for c in range(BLOCK // CHUNK):
        first = pl.multiple_of((1 - block[0]) * BLOCK + c * CHUNK, CHUNK)
        ids = pl.ds(first, CHUNK)
        scores = mm(far_rows, q[:, ids])
        upper, lower = softmax_coef(scores, times, ends[1:2, ids], first, live[0])
        high[:, ids] = upper
        low[:, ids] = lower
        query_grad = mm(far[...], upper) + mm(far[...], lower)
        part = slice(c * CHUNK, (c + 1) * CHUNK)
        grad[:, part] = (query_grad * scale[:, part]).astype(BF16)
    for read in reads[4:]:
        read.wait()
    for c in range(far_grad.shape[1] // CHUNK):
        part = slice(c * CHUNK, (c + 1) * CHUNK)
        both = mm(q[...], high[part, :], NT) + mm(q[...], low[part, :], NT)
        far_grad[:, part] = dithered(both)


def update_entities(
    block, ends, state, home, ent_hbm, grad_a, grad_b, new_state, new_hbm,
    ent, grad, new, sems,
):
    reads = [
        pltpu.make_async_copy(src, dst, sems.at[i])
        for i, (src, dst) in enumerate(
            [
                (grad_a, grad.at[:, block_lanes(block[0])]),
                (grad_b, grad.at[:, block_lanes(1 - block[0])]),
                (ent_hbm, ent),
            ]
        )
    ]
    for read in reads:
        read.start()
    for read in reads:
        read.wait()
    writes = []
    for c in range(ent.shape[1] // CHUNK):
        part = slice(c * CHUNK, (c + 1) * CHUNK)
        index = lax.broadcasted_iota(jnp.int32, (CHUNK, ends.shape[1]), 0) + c * CHUNK
        chosen = jnp.where(index == ends[0:1, :], 1.0, 0.0).astype(BF16)
        total = mm(grad[...], chosen, NT) + home[:, part].astype(F32)
        updated = state[0:1, part] + jnp.mean(total * total, axis=0, keepdims=True)
        new_state[0:1, part] = updated
        new[:, part] = ent[:, part] - entity_rate * total / jnp.sqrt(updated)
        write = pltpu.make_async_copy(new.at[:, part], new_hbm.at[:, part], sems.at[3 + c])
        write.start()
        writes.append(write)
    for write in writes:
        write.wait()


def sum_spread(pieces, out):
    out[...] = jnp.broadcast_to(jnp.sum(pieces[...], axis=0, keepdims=True), out.shape)


def update_relations(pieces, rel, state, out):
    total = jnp.sum(pieces[...], axis=0)
    updated = state[...] + jnp.mean(total * total, axis=1, keepdims=True)
    new = rel[...] - relation_rate * total / jnp.sqrt(updated)
    out[...] = jnp.broadcast_to(new[None], out.shape)


def call(kernel, args, outs, spaces, out_spaces, scratch=()):
    def spec(space, shape):
        if space == "b":
            return pl.BlockSpec(shape, lambda: (0,) * len(shape))
        return pl.BlockSpec(memory_space={"s": pltpu.SMEM, "v": pltpu.VMEM, "h": pltpu.HBM}[space])

    args = [
        pltpu.with_memory_space_constraint(arg, pltpu.HBM) if space in "hb" else arg
        for space, arg in zip(spaces, args, strict=True)
    ]
    return pl.pallas_call(
        kernel,
        out_shape=[
            pltpu.HBM(out.shape, out.dtype) if space in "hb" else out
            for space, out in zip(out_spaces, outs, strict=True)
        ],
        in_specs=[spec(space, arg.shape) for space, arg in zip(spaces, args, strict=True)],
        out_specs=[spec(space, out.shape) for space, out in zip(out_spaces, outs, strict=True)],
        scratch_shapes=list(scratch),
        compiler_params=pltpu.CompilerParams(vmem_limit_bytes=24 << 20),
    )(*args)


def passed_along(block, axis, distance):
    size = lax.axis_size(axis)
    return lax.ppermute(block, axis, [((i - distance) % size, i) for i in range(size)])


def mesh_groups():
    n_bucket, n_depth = lax.axis_size("bucket"), lax.axis_size("depth")
    n_x, n_y, n_core = 4, lax.axis_size("dom") // 8, 2

    def dom(x, y, core):
        return (x * n_y + y) * n_core + core

    along = [
        [dom(x, y, core) * n_bucket + z for y in range(n_y) for z in range(n_bucket)]
        for x in range(n_x)
        for core in range(n_core)
    ]
    across = [
        [
            dom(x, y, core) * n_depth + k
            for x in range(n_x)
            for core in range(n_core)
            for k in range(n_depth)
        ]
        for y in range(n_y)
    ]
    place = (lax.axis_index("dom") // n_core % n_y) * n_bucket + lax.axis_index("bucket")
    return along, across, place


def local(
    entities, entity_state, relations, relation_state, edge_ends, relation_ids, neg_ids, edge_count
):
    half_dom = lax.axis_size("dom") // 2
    rows, width = entities.shape
    n_rel = relations.shape[0]
    edges = relation_ids.shape[0]
    shape = jax.ShapeDtypeStruct
    rid = relation_ids.reshape(1, edges)

    neg_other = passed_along(neg_ids, "depth", 1)
    own = entities.T.astype(BF16)
    far = passed_along(own, "dom", half_dom)

    blocks = neg_ids.shape[0]
    wide, narrow = (width, edges), (width, BLOCK)
    q, left, scale, count = call(
        prepare,
        (own, relations.T, edge_ends, rid, neg_ids, neg_other),
        (shape(wide, BF16), shape(wide, BF16), shape(wide, F32), shape((blocks, rows, 128), F32)),
        "vvvvvv",
        "bbbb",
    )
    mine = lax.axis_index("depth").astype(jnp.int32).reshape(1)
    mat = (rows, BLOCK)
    high, low, grad_a, rel_grad = call(
        own_block,
        (mine, edge_count, edge_ends, rid, far, q, left, scale, count),
        (shape(mat, BF16), shape(mat, BF16), shape(narrow, BF16), shape((n_rel, width), F32)),
        "ssvvvhhhh",
        "hhhb",
        (
            pltpu.VMEM(narrow, BF16),
            pltpu.VMEM(narrow, BF16),
            pltpu.VMEM(narrow, F32),
            pltpu.VMEM((rows, 128), F32),
            pltpu.VMEM(mat, BF16),
            pltpu.VMEM(mat, BF16),
            pltpu.VMEM(narrow, BF16),
            pltpu.SemaphoreType.DMA((10,)),
        ),
    )
    along, across, place = mesh_groups()
    groups = len(along[0])
    share = n_rel // groups

    def exchange(pieces, axis, index_groups):
        return lax.all_to_all(pieces, axis, 0, 0, axis_index_groups=index_groups)

    pieces = exchange(rel_grad.reshape(groups, share, width), ("dom", "bucket"), along)

    far_grad, grad_b = call(
        other_block,
        (mine, edge_count, edge_ends, far, q, scale, count, high, low),
        (shape((width, rows), BF16), shape(narrow, BF16)),
        "ssvhhhhhh",
        "vb",
        (
            pltpu.VMEM((width, rows), BF16),
            pltpu.VMEM(wide, BF16),
            pltpu.VMEM(narrow, F32),
            pltpu.VMEM((rows, 128), F32),
            pltpu.VMEM((rows, edges), BF16),
            pltpu.VMEM((rows, edges), BF16),
            pltpu.SemaphoreType.DMA((6,)),
        ),
    )
    home_grad = passed_along(far_grad, "dom", half_dom)

    first = place * share
    my_rel = lax.dynamic_slice_in_dim(relations, first, share, 0)
    my_state = lax.dynamic_slice_in_dim(relation_state, first, share, 0)[:, None]
    pieces, far_grad = lax.optimization_barrier((pieces, far_grad))
    stack = (shape((len(across[0]), share, width), F32),)
    (partial,) = call(sum_spread, (pieces,), stack, "v", "b")
    totals = exchange(partial, ("dom", "depth"), across)
    stack = (shape((groups, share, width), F32),)
    (new_rel,) = call(update_relations, (totals, my_rel, my_state), stack, "vvv", "b")
    new_relations = exchange(new_rel, ("dom", "bucket"), along).reshape(n_rel, width)

    new_state, new_entities = call(
        update_entities,
        (mine, edge_ends, entity_state.reshape(1, rows), home_grad, entities.T, grad_a, grad_b),
        (shape((1, rows), F32), shape((width, rows), F32)),
        "svvvhhh",
        "vh",
        (
            pltpu.VMEM((width, rows), F32),
            pltpu.VMEM(wide, BF16),
            pltpu.VMEM((width, rows), F32),
            pltpu.SemaphoreType.DMA((7,)),
        ),
    )
    return (new_entities.T, new_state.reshape(rows), new_relations)


def solution(mesh):
    return jax.shard_map(
        local,
        mesh=mesh,
        in_specs=(
            P(("dom", "bucket"), None),
            P(("dom", "bucket")),
            P(),
            P(),
            P(None, ("dom", "bucket")),
            P(("dom", "bucket")),
            P(("dom", "bucket"), "depth"),
            P(("dom", "bucket")),
        ),
        out_specs=(P(("dom", "bucket"), None), P(("dom", "bucket")), P()),
        check_vma=False,
    )
```

```python
import jax
import jax.numpy as jnp
from jax import lax
from jax.experimental import pallas as pl
from jax.experimental.pallas import tpu as pltpu
from jax.sharding import PartitionSpec as P

BLOCK = 512

entity_rate = 0.1
relation_rate = 1.0

F32 = jnp.float32
BF16 = jnp.bfloat16
NN = (((1,), (0,)), ((), ()))
NT = (((1,), (1,)), ((), ()))


def mm(a, b, dims=NN):
    return lax.dot_general(a, b, dims, preferred_element_type=F32)


def onehot(ids, rows):
    index = lax.broadcasted_iota(jnp.int32, (rows, ids.shape[1]), 0)
    return jnp.where(index == ids, 1.0, 0.0).astype(BF16)


def split(value, parts):
    out = []
    for _ in range(parts):
        piece = value.astype(BF16)
        out.append(piece)
        value = value - piece.astype(F32)
    return out


def prepare(own, rel, ends, rid, neg_a, neg_b, q, left, scale, count):
    rel_parts = split(rel[...], 3)
    ones = jnp.ones((neg_a.shape[1], 128), BF16)
    for c in range(q.shape[1] // BLOCK):
        lanes = slice(c * BLOCK, (c + 1) * BLOCK)
        picked = mm(own[...], onehot(ends[0:1, lanes], own.shape[1]))
        by_rel = onehot(rid[0:1, lanes], rel.shape[1])
        factor = sum(mm(part, by_rel) for part in rel_parts)
        q[:, lanes] = (picked * factor).astype(BF16)
        left[:, lanes] = picked.astype(BF16)
        scale[:, lanes] = factor
        hits = mm(onehot(neg_a[c : c + 1, :], own.shape[1]), ones)
        count[c] = hits + mm(onehot(neg_b[c : c + 1, :], own.shape[1]), ones)


CHUNK = 512
TILE = 256


def block_lanes(block):
    return pl.ds(pl.multiple_of(block * BLOCK, BLOCK), BLOCK)


def softmax_coef(scores, times, right_ids, first, live):
    right = lax.broadcasted_iota(jnp.int32, scores.shape, 0) == right_ids
    positive = jnp.sum(jnp.where(right, scores, 0.0), axis=0, keepdims=True)
    masked = jnp.where(times > 0.0, scores, -3.0e38)
    peak = jnp.maximum(positive, jnp.max(masked, axis=0, keepdims=True))
    shifted = jnp.exp(masked - peak)
    top = jnp.exp(positive - peak)
    denom = top + jnp.sum(shifted * times, axis=0, keepdims=True)
    slot = lax.broadcasted_iota(jnp.int32, right_ids.shape, 1) + first
    active = jnp.where(slot < live, 1.0, 0.0)
    pos_coef = active * (top / denom - 1.0)
    weights = (shifted * (active / denom)).astype(BF16).astype(F32) * times
    return split(weights + jnp.where(right, pos_coef, 0.0), 2)


def own_block(
    block, live, ends, rid, far, q, left, scale, count,
    high_hbm, low_hbm, grad_hbm, rel_hbm,
    high, low, grad, rel_grad, sems,
):
    far_rows = far[...].T
    times = jnp.tile(count[block[0]], (1, CHUNK // 128))
    total, writes = None, []
    for c in range(BLOCK // CHUNK):
        part = slice(c * CHUNK, (c + 1) * CHUNK)
        first = pl.multiple_of(block[0] * BLOCK + c * CHUNK, CHUNK)
        ids = pl.ds(first, CHUNK)
        scores = mm(far_rows, q[:, ids])
        upper, lower = softmax_coef(scores, times, ends[1:2, ids], first, live[0])
        high[:, part] = upper
        low[:, part] = lower
        query_grad = mm(far[...], upper) + mm(far[...], lower)
        grad[:, part] = (query_grad * scale[:, ids]).astype(BF16)
        for i, (src, dst) in enumerate([(high, high_hbm), (low, low_hbm), (grad, grad_hbm)]):
            write = pltpu.make_async_copy(
                src.at[:, part], dst.at[:, part], sems.at[3 * c + i]
            )
            write.start()
            writes.append(write)
        pieces = split(query_grad * left[:, ids].astype(F32), 2)
        by_rel = onehot(rid[0:1, ids], rel_grad.shape[0])
        share = mm(by_rel, pieces[0], NT) + mm(by_rel, pieces[1], NT)
        total = share if total is None else total + share
    rel_grad[...] = total
    write = pltpu.make_async_copy(rel_grad, rel_hbm, sems.at[3 * (BLOCK // CHUNK)])
    write.start()
    writes.append(write)
    for write in writes:
        write.wait()


def dithered(value):
    row = lax.broadcasted_iota(jnp.int32, (value.shape[0], 1), 0).astype(F32) * 0.61803398875
    shift = (row - jnp.floor(row) - 0.5) * (1.0 / 256.0)
    return (value + value * shift).astype(BF16)


def other_block(
    block, live, ends, far_hbm, q_hbm, scale_hbm, count_hbm, high_hbm, low_hbm,
    far_grad, grad,
    far, q, scale, count, high, low, sems,
):
    lanes = block_lanes(1 - block[0])
    done = block_lanes(block[0])
    reads = [
        pltpu.make_async_copy(src, dst, sems.at[i])
        for i, (src, dst) in enumerate(
            [
                (far_hbm, far),
                (q_hbm, q),
                (count_hbm.at[1 - block[0]], count),
                (scale_hbm.at[:, lanes], scale),
                (high_hbm, high.at[:, done]),
                (low_hbm, low.at[:, done]),
            ]
        )
    ]
    for read in reads:
        read.start()
    for read in reads[:4]:
        read.wait()
    far_rows = far[...].T
    times = jnp.tile(count[...], (1, CHUNK // 128))
    for c in range(BLOCK // CHUNK):
        first = pl.multiple_of((1 - block[0]) * BLOCK + c * CHUNK, CHUNK)
        ids = pl.ds(first, CHUNK)
        scores = mm(far_rows, q[:, ids])
        upper, lower = softmax_coef(scores, times, ends[1:2, ids], first, live[0])
        high[:, ids] = upper
        low[:, ids] = lower
        query_grad = mm(far[...], upper) + mm(far[...], lower)
        part = slice(c * CHUNK, (c + 1) * CHUNK)
        grad[:, part] = (query_grad * scale[:, part]).astype(BF16)
    for read in reads[4:]:
        read.wait()
    for c in range(far_grad.shape[1] // TILE):
        part = slice(c * TILE, (c + 1) * TILE)
        both = mm(q[...], high[part, :], NT) + mm(q[...], low[part, :], NT)
        far_grad[:, part] = dithered(both)


def update_entities(
    block, ends, state, home, ent_hbm, grad_a, grad_b, new_state, new_hbm,
    ent, grad, new, sems,
):
    reads = [
        pltpu.make_async_copy(src, dst, sems.at[i])
        for i, (src, dst) in enumerate(
            [
                (grad_a, grad.at[:, block_lanes(block[0])]),
                (grad_b, grad.at[:, block_lanes(1 - block[0])]),
                (ent_hbm, ent),
            ]
        )
    ]
    for read in reads:
        read.start()
    for read in reads:
        read.wait()
    writes = []
    for c in range(ent.shape[1] // TILE):
        part = slice(c * TILE, (c + 1) * TILE)
        index = lax.broadcasted_iota(jnp.int32, (TILE, ends.shape[1]), 0) + c * TILE
        chosen = jnp.where(index == ends[0:1, :], 1.0, 0.0).astype(BF16)
        total = mm(grad[...], chosen, NT) + home[:, part].astype(F32)
        updated = state[0:1, part] + jnp.mean(total * total, axis=0, keepdims=True)
        new_state[0:1, part] = updated
        new[:, part] = ent[:, part] - entity_rate * total / jnp.sqrt(updated)
        write = pltpu.make_async_copy(new.at[:, part], new_hbm.at[:, part], sems.at[3 + c])
        write.start()
        writes.append(write)
    for write in writes:
        write.wait()


def sum_spread(pieces, out):
    out[...] = jnp.broadcast_to(jnp.sum(pieces[...], axis=0, keepdims=True), out.shape)


def update_relations(pieces, rel, state, out):
    total = jnp.sum(pieces[...], axis=0)
    updated = state[...] + jnp.mean(total * total, axis=1, keepdims=True)
    new = rel[...] - relation_rate * total / jnp.sqrt(updated)
    out[...] = jnp.broadcast_to(new[None], out.shape)


def call(kernel, args, outs, spaces, out_spaces, scratch=()):
    def spec(space, shape):
        if space == "b":
            return pl.BlockSpec(shape, lambda: (0,) * len(shape))
        return pl.BlockSpec(memory_space={"s": pltpu.SMEM, "v": pltpu.VMEM, "h": pltpu.HBM}[space])

    args = [
        pltpu.with_memory_space_constraint(arg, pltpu.HBM) if space in "hb" else arg
        for space, arg in zip(spaces, args, strict=True)
    ]
    return pl.pallas_call(
        kernel,
        out_shape=[
            pltpu.HBM(out.shape, out.dtype) if space in "hb" else out
            for space, out in zip(out_spaces, outs, strict=True)
        ],
        in_specs=[spec(space, arg.shape) for space, arg in zip(spaces, args, strict=True)],
        out_specs=[spec(space, out.shape) for space, out in zip(out_spaces, outs, strict=True)],
        scratch_shapes=list(scratch),
        compiler_params=pltpu.CompilerParams(vmem_limit_bytes=24 << 20),
    )(*args)


def passed_along(block, axis, distance):
    size = lax.axis_size(axis)
    return lax.ppermute(block, axis, [((i - distance) % size, i) for i in range(size)])


def mesh_groups():
    n_bucket, n_depth = lax.axis_size("bucket"), lax.axis_size("depth")
    n_x, n_y, n_core = 4, lax.axis_size("dom") // 8, 2

    def dom(x, y, core):
        return (x * n_y + y) * n_core + core

    along = [
        [dom(x, y, core) * n_bucket + z for y in range(n_y) for z in range(n_bucket)]
        for x in range(n_x)
        for core in range(n_core)
    ]
    across = [
        [
            dom(x, y, core) * n_depth + k
            for x in range(n_x)
            for core in range(n_core)
            for k in range(n_depth)
        ]
        for y in range(n_y)
    ]
    place = (lax.axis_index("dom") // n_core % n_y) * n_bucket + lax.axis_index("bucket")
    return along, across, place


def local(
    entities, entity_state, relations, relation_state, edge_ends, relation_ids, neg_ids, edge_count
):
    half_dom = lax.axis_size("dom") // 2
    rows, width = entities.shape
    n_rel = relations.shape[0]
    edges = relation_ids.shape[0]
    shape = jax.ShapeDtypeStruct
    rid = relation_ids.reshape(1, edges)

    neg_other = passed_along(neg_ids, "depth", 1)
    own = entities.T.astype(BF16)
    far = passed_along(own, "dom", half_dom)

    blocks = neg_ids.shape[0]
    wide, narrow = (width, edges), (width, BLOCK)
    q, left, scale, count = call(
        prepare,
        (own, relations.T, edge_ends, rid, neg_ids, neg_other),
        (shape(wide, BF16), shape(wide, BF16), shape(wide, F32), shape((blocks, rows, 128), F32)),
        "vvvvvv",
        "vvvv",
    )
    mine = lax.axis_index("depth").astype(jnp.int32).reshape(1)
    mat = (rows, BLOCK)
    high, low, grad_a, rel_grad = call(
        own_block,
        (mine, edge_count, edge_ends, rid, far, q, left, scale, count),
        (shape(mat, BF16), shape(mat, BF16), shape(narrow, BF16), shape((n_rel, width), F32)),
        "ssvvvvvvv",
        "hhhh",
        (
            pltpu.VMEM(mat, BF16),
            pltpu.VMEM(mat, BF16),
            pltpu.VMEM(narrow, BF16),
            pltpu.VMEM((n_rel, width), F32),
            pltpu.SemaphoreType.DMA((3 * (BLOCK // CHUNK) + 1,)),
        ),
    )
    along, across, place = mesh_groups()
    groups = len(along[0])
    share = n_rel // groups

    def exchange(pieces, axis, index_groups):
        return lax.all_to_all(pieces, axis, 0, 0, axis_index_groups=index_groups)

    pieces = exchange(rel_grad.reshape(groups, share, width), ("dom", "bucket"), along)

    far_grad, grad_b = call(
        other_block,
        (mine, edge_count, edge_ends, far, q, scale, count, high, low),
        (shape((width, rows), BF16), shape(narrow, BF16)),
        "ssvhhhhhh",
        "vb",
        (
            pltpu.VMEM((width, rows), BF16),
            pltpu.VMEM(wide, BF16),
            pltpu.VMEM(narrow, F32),
            pltpu.VMEM((rows, 128), F32),
            pltpu.VMEM((rows, edges), BF16),
            pltpu.VMEM((rows, edges), BF16),
            pltpu.SemaphoreType.DMA((6,)),
        ),
    )
    home_grad = passed_along(far_grad, "dom", half_dom)

    first = place * share
    my_rel = lax.dynamic_slice_in_dim(relations, first, share, 0)
    my_state = lax.dynamic_slice_in_dim(relation_state, first, share, 0)[:, None]
    pieces, far_grad = lax.optimization_barrier((pieces, far_grad))
    stack = (shape((len(across[0]), share, width), F32),)
    (partial,) = call(sum_spread, (pieces,), stack, "v", "b")
    totals = exchange(partial, ("dom", "depth"), across)
    stack = (shape((groups, share, width), F32),)
    (new_rel,) = call(update_relations, (totals, my_rel, my_state), stack, "vvv", "b")
    new_relations = exchange(new_rel, ("dom", "bucket"), along).reshape(n_rel, width)

    new_state, new_entities = call(
        update_entities,
        (mine, edge_ends, entity_state.reshape(1, rows), home_grad, entities.T, grad_a, grad_b),
        (shape((1, rows), F32), shape((width, rows), F32)),
        "svvvhhh",
        "vh",
        (
            pltpu.VMEM((width, rows), F32),
            pltpu.VMEM(wide, BF16),
            pltpu.VMEM((width, rows), F32),
            pltpu.SemaphoreType.DMA((7,)),
        ),
    )
    return (new_entities.T, new_state.reshape(rows), new_relations)


def solution(mesh):
    return jax.shard_map(
        local,
        mesh=mesh,
        in_specs=(
            P(("dom", "bucket"), None),
            P(("dom", "bucket")),
            P(),
            P(),
            P(None, ("dom", "bucket")),
            P(("dom", "bucket")),
            P(("dom", "bucket"), "depth"),
            P(("dom", "bucket")),
        ),
        out_specs=(P(("dom", "bucket"), None), P(("dom", "bucket")), P()),
        check_vma=False,
    )
```

```python
import jax
import jax.numpy as jnp
from jax import lax
from jax.experimental import pallas as pl
from jax.experimental.pallas import tpu as pltpu
from jax.sharding import PartitionSpec as P

BLOCK = 512


entity_rate = 0.1
relation_rate = 1.0

F32 = jnp.float32
BF16 = jnp.bfloat16
NN = (((1,), (0,)), ((), ()))
NT = (((1,), (1,)), ((), ()))


def mm(a, b, dims=NN):
    return lax.dot_general(a, b, dims, preferred_element_type=F32)


def onehot(ids, rows):
    index = lax.broadcasted_iota(jnp.int32, (rows, ids.shape[1]), 0)
    return jnp.where(index == ids, 1.0, 0.0).astype(BF16)


def split(value, parts):
    out = []
    for _ in range(parts):
        piece = value.astype(BF16)
        out.append(piece)
        value = value - piece.astype(F32)
    return out


def prepare(entities, rel, ends, rid, neg_a, neg_b, q, left, scale, count):
    own = entities[...].astype(BF16)
    rel_parts = split(rel[...], 3)
    ones = jnp.ones((neg_a.shape[1], 128), BF16)
    for c in range(q.shape[1] // BLOCK):
        lanes = slice(c * BLOCK, (c + 1) * BLOCK)
        picked = mm(own, onehot(ends[0:1, lanes], own.shape[1]))
        by_rel = onehot(rid[0:1, lanes], rel.shape[1])
        factor = sum(mm(part, by_rel) for part in rel_parts)
        q[:, lanes] = (picked * factor).astype(BF16)
        left[:, lanes] = picked.astype(BF16)
        scale[:, lanes] = factor
        hits = mm(onehot(neg_a[c : c + 1, :], own.shape[1]), ones)
        count[c] = hits + mm(onehot(neg_b[c : c + 1, :], own.shape[1]), ones)


CHUNK = 512
TILE = 256


def block_lanes(block):
    return pl.ds(pl.multiple_of(block * BLOCK, BLOCK), BLOCK)


def softmax_coef(scores, times, right_ids, first, live):
    right = lax.broadcasted_iota(jnp.int32, scores.shape, 0) == right_ids
    positive = jnp.sum(jnp.where(right, scores, 0.0), axis=0, keepdims=True)
    masked = jnp.where(times > 0.0, scores, -3.0e38)
    peak = jnp.maximum(positive, jnp.max(masked, axis=0, keepdims=True))
    shifted = jnp.exp(masked - peak)
    top = jnp.exp(positive - peak)
    denom = top + jnp.sum(shifted * times, axis=0, keepdims=True)
    slot = lax.broadcasted_iota(jnp.int32, right_ids.shape, 1) + first
    active = jnp.where(slot < live, 1.0, 0.0)
    pos_coef = active * (top / denom - 1.0)
    weights = (shifted * (active / denom)).astype(BF16).astype(F32) * times
    return split(weights + jnp.where(right, pos_coef, 0.0), 2)


def own_block(
    block, live, ends, rid, outer, middle, peer, q, left, scale, count,
    high_hbm, low_hbm, grad_hbm, rel_hbm, far_hbm,
    high, low, grad, rel_grad, far, sems,
):
    edge, rest = outer.shape[1], far.shape[1] - outer.shape[1]
    far[:, pl.ds(pl.multiple_of(block[0] * rest, edge), edge)] = outer[...]
    far[:, edge:rest] = middle[...]
    far[:, pl.ds(pl.multiple_of((1 - block[0]) * rest, edge), edge)] = peer[...]
    keep = pltpu.make_async_copy(far, far_hbm, sems.at[3 * (BLOCK // CHUNK) + 1])
    keep.start()
    far_rows = far[...].T
    times = jnp.tile(count[block[0]], (1, CHUNK // 128))
    total, writes = None, [keep]
    for c in range(BLOCK // CHUNK):
        part = slice(c * CHUNK, (c + 1) * CHUNK)
        first = pl.multiple_of(block[0] * BLOCK + c * CHUNK, CHUNK)
        ids = pl.ds(first, CHUNK)
        scores = mm(far_rows, q[:, ids])
        upper, lower = softmax_coef(scores, times, ends[1:2, ids], first, live[0])
        high[:, part] = upper
        low[:, part] = lower
        query_grad = mm(far[...], upper) + mm(far[...], lower)
        grad[:, part] = (query_grad * scale[:, ids]).astype(BF16)
        for i, (src, dst) in enumerate([(high, high_hbm), (low, low_hbm), (grad, grad_hbm)]):
            write = pltpu.make_async_copy(
                src.at[:, part], dst.at[:, part], sems.at[3 * c + i]
            )
            write.start()
            writes.append(write)
        pieces = split(query_grad * left[:, ids].astype(F32), 2)
        by_rel = onehot(rid[0:1, ids], rel_grad.shape[0])
        share = mm(by_rel, pieces[0], NT) + mm(by_rel, pieces[1], NT)
        total = share if total is None else total + share
    rel_grad[...] = total
    write = pltpu.make_async_copy(rel_grad, rel_hbm, sems.at[3 * (BLOCK // CHUNK)])
    write.start()
    writes.append(write)
    for write in writes:
        write.wait()


def dithered(value):
    row = lax.broadcasted_iota(jnp.int32, (value.shape[0], 1), 0).astype(F32) * 0.61803398875
    shift = (row - jnp.floor(row) - 0.5) * (1.0 / 256.0)
    return (value + value * shift).astype(BF16)


def other_block(
    block, live, ends, far_hbm, q_hbm, scale_hbm, count_hbm, high_hbm, low_hbm,
    far_grad, grad,
    far, q, scale, count, high, low, sems,
):
    lanes = block_lanes(1 - block[0])
    done = block_lanes(block[0])
    reads = [
        pltpu.make_async_copy(src, dst, sems.at[i])
        for i, (src, dst) in enumerate(
            [
                (far_hbm, far),
                (q_hbm, q),
                (count_hbm.at[1 - block[0]], count),
                (scale_hbm.at[:, lanes], scale),
                (high_hbm, high.at[:, done]),
                (low_hbm, low.at[:, done]),
            ]
        )
    ]
    for read in reads:
        read.start()
    for read in reads[:4]:
        read.wait()
    far_rows = far[...].T
    times = jnp.tile(count[...], (1, CHUNK // 128))
    for c in range(BLOCK // CHUNK):
        first = pl.multiple_of((1 - block[0]) * BLOCK + c * CHUNK, CHUNK)
        ids = pl.ds(first, CHUNK)
        scores = mm(far_rows, q[:, ids])
        upper, lower = softmax_coef(scores, times, ends[1:2, ids], first, live[0])
        high[:, ids] = upper
        low[:, ids] = lower
        query_grad = mm(far[...], upper) + mm(far[...], lower)
        part = slice(c * CHUNK, (c + 1) * CHUNK)
        grad[:, part] = (query_grad * scale[:, part]).astype(BF16)
    for read in reads[4:]:
        read.wait()
    for c in range(far_grad.shape[1] // TILE):
        part = slice(c * TILE, (c + 1) * TILE)
        both = mm(q[...], high[part, :], NT) + mm(q[...], low[part, :], NT)
        far_grad[:, part] = dithered(both)


def update_entities(
    block, ends, state, home, ent_hbm, grad_a, grad_b, new_state, new_hbm,
    ent, grad, new, sems,
):
    reads = [
        pltpu.make_async_copy(src, dst, sems.at[i])
        for i, (src, dst) in enumerate(
            [
                (grad_a, grad.at[:, block_lanes(block[0])]),
                (grad_b, grad.at[:, block_lanes(1 - block[0])]),
                (ent_hbm, ent),
            ]
        )
    ]
    for read in reads:
        read.start()
    for read in reads:
        read.wait()
    writes = []
    for c in range(ent.shape[1] // TILE):
        part = slice(c * TILE, (c + 1) * TILE)
        index = lax.broadcasted_iota(jnp.int32, (TILE, ends.shape[1]), 0) + c * TILE
        chosen = jnp.where(index == ends[0:1, :], 1.0, 0.0).astype(BF16)
        total = mm(grad[...], chosen, NT) + home[:, part].astype(F32)
        updated = state[0:1, part] + jnp.mean(total * total, axis=0, keepdims=True)
        new_state[0:1, part] = updated
        new[:, part] = ent[:, part] - entity_rate * total / jnp.sqrt(updated)
        write = pltpu.make_async_copy(new.at[:, part], new_hbm.at[:, part], sems.at[3 + c])
        write.start()
        writes.append(write)
    for write in writes:
        write.wait()


def sum_spread(pieces, out):
    out[...] = jnp.broadcast_to(jnp.sum(pieces[...], axis=0, keepdims=True), out.shape)


def update_relations(pieces, rel, state, out):
    total = jnp.sum(pieces[...], axis=0)
    updated = state[...] + jnp.mean(total * total, axis=1, keepdims=True)
    new = rel[...] - relation_rate * total / jnp.sqrt(updated)
    out[...] = jnp.broadcast_to(new[None], out.shape)


def call(kernel, args, outs, spaces, out_spaces, scratch=()):
    def spec(space, shape):
        if space == "b":
            return pl.BlockSpec(shape, lambda: (0,) * len(shape))
        return pl.BlockSpec(memory_space={"s": pltpu.SMEM, "v": pltpu.VMEM, "h": pltpu.HBM}[space])

    args = [
        pltpu.with_memory_space_constraint(arg, pltpu.HBM) if space in "hb" else arg
        for space, arg in zip(spaces, args, strict=True)
    ]
    return pl.pallas_call(
        kernel,
        out_shape=[
            pltpu.HBM(out.shape, out.dtype) if space in "hb" else out
            for space, out in zip(out_spaces, outs, strict=True)
        ],
        in_specs=[spec(space, arg.shape) for space, arg in zip(spaces, args, strict=True)],
        out_specs=[spec(space, out.shape) for space, out in zip(out_spaces, outs, strict=True)],
        scratch_shapes=list(scratch),
        compiler_params=pltpu.CompilerParams(vmem_limit_bytes=24 << 20),
    )(*args)


def passed_along(block, axis, distance):
    size = lax.axis_size(axis)
    return lax.ppermute(block, axis, [((i - distance) % size, i) for i in range(size)])


def mesh_groups():
    n_bucket, n_depth = lax.axis_size("bucket"), lax.axis_size("depth")
    n_x, n_y, n_core = 4, lax.axis_size("dom") // 8, 2

    def dom(x, y, core):
        return (x * n_y + y) * n_core + core

    along = [
        [dom(x, y, core) * n_bucket + z for y in range(n_y) for z in range(n_bucket)]
        for x in range(n_x)
        for core in range(n_core)
    ]
    across = [
        [
            dom(x, y, core) * n_depth + k
            for x in range(n_x)
            for core in range(n_core)
            for k in range(n_depth)
        ]
        for y in range(n_y)
    ]
    place = (lax.axis_index("dom") // n_core % n_y) * n_bucket + lax.axis_index("bucket")
    return along, across, place


def local(
    entities, entity_state, relations, relation_state, edge_ends, relation_ids, neg_ids, edge_count
):
    half_dom = lax.axis_size("dom") // 2
    rows, width = entities.shape
    n_rel = relations.shape[0]
    edges = relation_ids.shape[0]
    shape = jax.ShapeDtypeStruct
    rid = relation_ids.reshape(1, edges)

    neg_other = passed_along(neg_ids, "depth", 1)
    depth = lax.axis_index("depth").astype(jnp.int32)
    edge = rows // 4
    outer = lax.dynamic_slice_in_dim(entities.T, depth * (rows - edge), edge, 1).astype(BF16)
    outer = passed_along(outer, "dom", half_dom)
    middle = entities.T[:, edge : rows - edge].astype(BF16)
    middle = passed_along(middle, "dom", half_dom)
    peer = passed_along(outer, "depth", 1)
    own, outer = lax.optimization_barrier((entities.T, outer))

    blocks = neg_ids.shape[0]
    wide, narrow = (width, edges), (width, BLOCK)
    q, left, scale, count = call(
        prepare,
        (own, relations.T, edge_ends, rid, neg_ids, neg_other),
        (shape(wide, BF16), shape(wide, BF16), shape(wide, F32), shape((blocks, rows, 128), F32)),
        "bbbbbv",
        "vvvv",
    )
    mine = depth.reshape(1)
    mat = (rows, BLOCK)
    high, low, grad_a, rel_grad, far = call(
        own_block,
        (mine, edge_count, edge_ends, rid, outer, middle, peer, q, left, scale, count),
        (
            shape(mat, BF16),
            shape(mat, BF16),
            shape(narrow, BF16),
            shape((n_rel, width), F32),
            shape((width, rows), BF16),
        ),
        "ssvvvvvvvvv",
        "hhhhh",
        (
            pltpu.VMEM(mat, BF16),
            pltpu.VMEM(mat, BF16),
            pltpu.VMEM(narrow, BF16),
            pltpu.VMEM((n_rel, width), F32),
            pltpu.VMEM((width, rows), BF16),
            pltpu.SemaphoreType.DMA((3 * (BLOCK // CHUNK) + 2,)),
        ),
    )
    along, across, place = mesh_groups()
    groups = len(along[0])
    share = n_rel // groups

    def exchange(pieces, axis, index_groups):
        return lax.all_to_all(pieces, axis, 0, 0, axis_index_groups=index_groups)

    pieces = exchange(rel_grad.reshape(groups, share, width), ("dom", "bucket"), along)

    far_grad, grad_b = call(
        other_block,
        (mine, edge_count, edge_ends, far, q, scale, count, high, low),
        (shape((width, rows), BF16), shape(narrow, BF16)),
        "ssvhhhhhh",
        "vb",
        (
            pltpu.VMEM((width, rows), BF16),
            pltpu.VMEM(wide, BF16),
            pltpu.VMEM(narrow, F32),
            pltpu.VMEM((rows, 128), F32),
            pltpu.VMEM((rows, edges), BF16),
            pltpu.VMEM((rows, edges), BF16),
            pltpu.SemaphoreType.DMA((6,)),
        ),
    )
    home_grad = passed_along(far_grad, "dom", half_dom)

    first = place * share
    my_rel = lax.dynamic_slice_in_dim(relations, first, share, 0)
    my_state = lax.dynamic_slice_in_dim(relation_state, first, share, 0)[:, None]
    pieces, far_grad = lax.optimization_barrier((pieces, far_grad))
    stack = (shape((len(across[0]), share, width), F32),)
    (partial,) = call(sum_spread, (pieces,), stack, "v", "b")
    totals = exchange(partial, ("dom", "depth"), across)
    stack = (shape((groups, share, width), F32),)
    (new_rel,) = call(update_relations, (totals, my_rel, my_state), stack, "vvv", "b")
    new_relations = exchange(new_rel, ("dom", "bucket"), along).reshape(n_rel, width)

    new_state, new_entities = call(
        update_entities,
        (mine, edge_ends, entity_state.reshape(1, rows), home_grad, entities.T, grad_a, grad_b),
        (shape((1, rows), F32), shape((width, rows), F32)),
        "svvvhhh",
        "vh",
        (
            pltpu.VMEM((width, rows), F32),
            pltpu.VMEM(wide, BF16),
            pltpu.VMEM((width, rows), F32),
            pltpu.SemaphoreType.DMA((7,)),
        ),
    )
    return (new_entities.T, new_state.reshape(rows), new_relations)


def solution(mesh):
    return jax.shard_map(
        local,
        mesh=mesh,
        in_specs=(
            P(("dom", "bucket"), None),
            P(("dom", "bucket")),
            P(),
            P(),
            P(None, ("dom", "bucket")),
            P(("dom", "bucket")),
            P(("dom", "bucket"), "depth"),
            P(("dom", "bucket")),
        ),
        out_specs=(P(("dom", "bucket"), None), P(("dom", "bucket")), P()),
        check_vma=False,
    )
```

```python
import jax
import jax.numpy as jnp
from jax import lax
from jax.experimental import pallas as pl
from jax.experimental.pallas import tpu as pltpu
from jax.sharding import PartitionSpec as P

BLOCK = 512


entity_rate = 0.1
relation_rate = 1.0

F32 = jnp.float32
BF16 = jnp.bfloat16
NN = (((1,), (0,)), ((), ()))
NT = (((1,), (1,)), ((), ()))


def mm(a, b, dims=NN):
    return lax.dot_general(a, b, dims, preferred_element_type=F32)


def onehot(ids, rows):
    index = lax.broadcasted_iota(jnp.int32, (rows, ids.shape[1]), 0)
    return jnp.where(index == ids, 1.0, 0.0).astype(BF16)


def split(value, parts):
    out = []
    for _ in range(parts):
        piece = value.astype(BF16)
        out.append(piece)
        value = value - piece.astype(F32)
    return out


def pack(depth, ent_hbm, outer, middle, own, ent, sems):
    edge, half = outer.shape[1], middle.shape[1]
    rest = own.shape[1] - edge
    first = pl.ds(pl.multiple_of(depth[0] * rest, edge), edge)
    last = pl.ds(pl.multiple_of((1 - depth[0]) * rest, edge), edge)
    reads = [
        pltpu.make_async_copy(ent_hbm.at[:, lanes], ent.at[:, lanes], sems.at[i])
        for i, lanes in enumerate([first, pl.ds(edge, half), last])
    ]
    for read in reads:
        read.start()
    reads[0].wait()
    piece = ent[:, first].astype(BF16)
    outer[...] = piece
    own[:, first] = piece
    reads[1].wait()
    piece = ent[:, edge:rest].astype(BF16)
    middle[...] = piece
    own[:, edge:rest] = piece
    reads[2].wait()
    own[:, last] = ent[:, last].astype(BF16)


def prepare(own, ends, rid, neg_a, neg_b, rel_hbm, q, left, scale, count, rel, sems):
    read = pltpu.make_async_copy(rel_hbm, rel, sems.at[0])
    read.start()
    ones = jnp.ones((neg_a.shape[1], 128), BF16)
    blocks = q.shape[1] // BLOCK
    for c in range(blocks):
        hits = mm(onehot(neg_a[c : c + 1, :], own.shape[1]), ones)
        count[c] = hits + mm(onehot(neg_b[c : c + 1, :], own.shape[1]), ones)
    read.wait()
    rel_parts = split(rel[...], 3)
    for c in range(blocks):
        lanes = slice(c * BLOCK, (c + 1) * BLOCK)
        picked = mm(own[...], onehot(ends[0:1, lanes], own.shape[1]))
        by_rel = onehot(rid[0:1, lanes], rel.shape[1])
        factor = sum(mm(part, by_rel) for part in rel_parts)
        q[:, lanes] = (picked * factor).astype(BF16)
        left[:, lanes] = picked.astype(BF16)
        scale[:, lanes] = factor


CHUNK = 512
TILE = 256


def block_lanes(block):
    return pl.ds(pl.multiple_of(block * BLOCK, BLOCK), BLOCK)


def softmax_coef(scores, times, right_ids, first, live):
    right = lax.broadcasted_iota(jnp.int32, scores.shape, 0) == right_ids
    positive = jnp.sum(jnp.where(right, scores, 0.0), axis=0, keepdims=True)
    masked = jnp.where(times > 0.0, scores, -3.0e38)
    peak = jnp.maximum(positive, jnp.max(masked, axis=0, keepdims=True))
    shifted = jnp.exp(masked - peak)
    top = jnp.exp(positive - peak)
    denom = top + jnp.sum(shifted * times, axis=0, keepdims=True)
    slot = lax.broadcasted_iota(jnp.int32, right_ids.shape, 1) + first
    active = jnp.where(slot < live, 1.0, 0.0)
    pos_coef = active * (top / denom - 1.0)
    weights = (shifted * (active / denom)).astype(BF16).astype(F32) * times
    return split(weights + jnp.where(right, pos_coef, 0.0), 2)


def own_block(
    block, live, ends, rid, outer, middle, peer, q, left, scale, count,
    high_hbm, low_hbm, grad_hbm, rel_hbm, far_hbm,
    high, low, grad, rel_grad, far, sems,
):
    edge, rest = outer.shape[1], far.shape[1] - outer.shape[1]
    far[:, pl.ds(pl.multiple_of(block[0] * rest, edge), edge)] = outer[...]
    far[:, edge:rest] = middle[...]
    far[:, pl.ds(pl.multiple_of((1 - block[0]) * rest, edge), edge)] = peer[...]
    keep = pltpu.make_async_copy(far, far_hbm, sems.at[3 * (BLOCK // CHUNK) + 1])
    keep.start()
    far_rows = far[...].T
    times = jnp.tile(count[block[0]], (1, CHUNK // 128))
    total, writes = None, [keep]
    for c in range(BLOCK // CHUNK):
        part = slice(c * CHUNK, (c + 1) * CHUNK)
        first = pl.multiple_of(block[0] * BLOCK + c * CHUNK, CHUNK)
        ids = pl.ds(first, CHUNK)
        scores = mm(far_rows, q[:, ids])
        upper, lower = softmax_coef(scores, times, ends[1:2, ids], first, live[0])
        high[:, part] = upper
        low[:, part] = lower
        query_grad = mm(far[...], upper) + mm(far[...], lower)
        grad[:, part] = (query_grad * scale[:, ids]).astype(BF16)
        for i, (src, dst) in enumerate([(high, high_hbm), (low, low_hbm), (grad, grad_hbm)]):
            write = pltpu.make_async_copy(
                src.at[:, part], dst.at[:, part], sems.at[3 * c + i]
            )
            write.start()
            writes.append(write)
        pieces = split(query_grad * left[:, ids].astype(F32), 2)
        by_rel = onehot(rid[0:1, ids], rel_grad.shape[0])
        share = mm(by_rel, pieces[0], NT) + mm(by_rel, pieces[1], NT)
        total = share if total is None else total + share
    rel_grad[...] = total
    write = pltpu.make_async_copy(rel_grad, rel_hbm, sems.at[3 * (BLOCK // CHUNK)])
    write.start()
    writes.append(write)
    for write in writes:
        write.wait()


def dithered(value):
    row = lax.broadcasted_iota(jnp.int32, (value.shape[0], 1), 0).astype(F32) * 0.61803398875
    shift = (row - jnp.floor(row) - 0.5) * (1.0 / 256.0)
    return (value + value * shift).astype(BF16)


def other_block(
    block, live, ends, far_hbm, q_hbm, scale_hbm, count_hbm, high_hbm, low_hbm,
    far_grad, grad,
    far, q, scale, count, high, low, sems,
):
    lanes = block_lanes(1 - block[0])
    done = block_lanes(block[0])
    reads = [
        pltpu.make_async_copy(src, dst, sems.at[i])
        for i, (src, dst) in enumerate(
            [
                (far_hbm, far),
                (q_hbm, q),
                (count_hbm.at[1 - block[0]], count),
                (scale_hbm.at[:, lanes], scale),
                (high_hbm, high.at[:, done]),
                (low_hbm, low.at[:, done]),
            ]
        )
    ]
    for read in reads:
        read.start()
    for read in reads[:4]:
        read.wait()
    far_rows = far[...].T
    times = jnp.tile(count[...], (1, CHUNK // 128))
    for c in range(BLOCK // CHUNK):
        first = pl.multiple_of((1 - block[0]) * BLOCK + c * CHUNK, CHUNK)
        ids = pl.ds(first, CHUNK)
        scores = mm(far_rows, q[:, ids])
        upper, lower = softmax_coef(scores, times, ends[1:2, ids], first, live[0])
        high[:, ids] = upper
        low[:, ids] = lower
        query_grad = mm(far[...], upper) + mm(far[...], lower)
        part = slice(c * CHUNK, (c + 1) * CHUNK)
        grad[:, part] = (query_grad * scale[:, part]).astype(BF16)
    for read in reads[4:]:
        read.wait()
    for c in range(far_grad.shape[1] // TILE):
        part = slice(c * TILE, (c + 1) * TILE)
        both = mm(q[...], high[part, :], NT) + mm(q[...], low[part, :], NT)
        far_grad[:, part] = dithered(both)


def update_entities(
    block, ends, state, home, ent_hbm, grad_a, grad_b, new_state, new_hbm,
    ent, grad, new, sems,
):
    reads = [
        pltpu.make_async_copy(src, dst, sems.at[i])
        for i, (src, dst) in enumerate(
            [
                (grad_a, grad.at[:, block_lanes(block[0])]),
                (grad_b, grad.at[:, block_lanes(1 - block[0])]),
                (ent_hbm, ent),
            ]
        )
    ]
    for read in reads:
        read.start()
    for read in reads:
        read.wait()
    writes = []
    for c in range(ent.shape[1] // TILE):
        part = slice(c * TILE, (c + 1) * TILE)
        index = lax.broadcasted_iota(jnp.int32, (TILE, ends.shape[1]), 0) + c * TILE
        chosen = jnp.where(index == ends[0:1, :], 1.0, 0.0).astype(BF16)
        total = mm(grad[...], chosen, NT) + home[:, part].astype(F32)
        updated = state[0:1, part] + jnp.mean(total * total, axis=0, keepdims=True)
        new_state[0:1, part] = updated
        new[:, part] = ent[:, part] - entity_rate * total / jnp.sqrt(updated)
        write = pltpu.make_async_copy(new.at[:, part], new_hbm.at[:, part], sems.at[3 + c])
        write.start()
        writes.append(write)
    for write in writes:
        write.wait()


def sum_spread(pieces, out):
    out[...] = jnp.broadcast_to(jnp.sum(pieces[...], axis=0, keepdims=True), out.shape)


def update_relations(pieces, rel, state, out):
    total = jnp.sum(pieces[...], axis=0)
    updated = state[...] + jnp.mean(total * total, axis=1, keepdims=True)
    new = rel[...] - relation_rate * total / jnp.sqrt(updated)
    out[...] = jnp.broadcast_to(new[None], out.shape)


def call(kernel, args, outs, spaces, out_spaces, scratch=()):
    def spec(space, shape):
        if space == "b":
            return pl.BlockSpec(shape, lambda: (0,) * len(shape))
        return pl.BlockSpec(memory_space={"s": pltpu.SMEM, "v": pltpu.VMEM, "h": pltpu.HBM}[space])

    args = [
        pltpu.with_memory_space_constraint(arg, pltpu.HBM) if space in "hb" else arg
        for space, arg in zip(spaces, args, strict=True)
    ]
    return pl.pallas_call(
        kernel,
        out_shape=[
            pltpu.HBM(out.shape, out.dtype) if space in "hb" else out
            for space, out in zip(out_spaces, outs, strict=True)
        ],
        in_specs=[spec(space, arg.shape) for space, arg in zip(spaces, args, strict=True)],
        out_specs=[spec(space, out.shape) for space, out in zip(out_spaces, outs, strict=True)],
        scratch_shapes=list(scratch),
        compiler_params=pltpu.CompilerParams(vmem_limit_bytes=24 << 20),
    )(*args)


def passed_along(block, axis, distance):
    size = lax.axis_size(axis)
    return lax.ppermute(block, axis, [((i - distance) % size, i) for i in range(size)])


def mesh_groups():
    n_bucket, n_depth = lax.axis_size("bucket"), lax.axis_size("depth")
    n_x, n_y, n_core = 4, lax.axis_size("dom") // 8, 2

    def dom(x, y, core):
        return (x * n_y + y) * n_core + core

    along = [
        [dom(x, y, core) * n_bucket + z for y in range(n_y) for z in range(n_bucket)]
        for x in range(n_x)
        for core in range(n_core)
    ]
    across = [
        [
            dom(x, y, core) * n_depth + k
            for x in range(n_x)
            for core in range(n_core)
            for k in range(n_depth)
        ]
        for y in range(n_y)
    ]
    place = (lax.axis_index("dom") // n_core % n_y) * n_bucket + lax.axis_index("bucket")
    return along, across, place


def local(
    entities, entity_state, relations, relation_state, edge_ends, relation_ids, neg_ids, edge_count
):
    half_dom = lax.axis_size("dom") // 2
    rows, width = entities.shape
    n_rel = relations.shape[0]
    edges = relation_ids.shape[0]
    shape = jax.ShapeDtypeStruct
    rid = relation_ids.reshape(1, edges)

    neg_other = passed_along(neg_ids, "depth", 1)
    depth = lax.axis_index("depth").astype(jnp.int32)
    edge = rows // 4
    mine = depth.reshape(1)
    outer, middle, own = call(
        pack,
        (mine, entities.T),
        (shape((width, edge), BF16), shape((width, rows - 2 * edge), BF16), shape((width, rows), BF16)),
        "sh",
        "vvv",
        (pltpu.VMEM((width, rows), F32), pltpu.SemaphoreType.DMA((3,))),
    )
    outer = passed_along(outer, "dom", half_dom)
    middle = passed_along(middle, "dom", half_dom)
    peer = passed_along(outer, "depth", 1)
    own, outer = lax.optimization_barrier((own, outer))

    blocks = neg_ids.shape[0]
    wide, narrow = (width, edges), (width, BLOCK)
    q, left, scale, count = call(
        prepare,
        (own, edge_ends, rid, neg_ids, neg_other, relations.T),
        (shape(wide, BF16), shape(wide, BF16), shape(wide, F32), shape((blocks, rows, 128), F32)),
        "vvvvvh",
        "vvvv",
        (pltpu.VMEM((width, n_rel), F32), pltpu.SemaphoreType.DMA((1,))),
    )
    mat = (rows, BLOCK)
    high, low, grad_a, rel_grad, far = call(
        own_block,
        (mine, edge_count, edge_ends, rid, outer, middle, peer, q, left, scale, count),
        (
            shape(mat, BF16),
            shape(mat, BF16),
            shape(narrow, BF16),
            shape((n_rel, width), F32),
            shape((width, rows), BF16),
        ),
        "ssvvvvvvvvv",
        "hhhhh",
        (
            pltpu.VMEM(mat, BF16),
            pltpu.VMEM(mat, BF16),
            pltpu.VMEM(narrow, BF16),
            pltpu.VMEM((n_rel, width), F32),
            pltpu.VMEM((width, rows), BF16),
            pltpu.SemaphoreType.DMA((3 * (BLOCK // CHUNK) + 2,)),
        ),
    )
    along, across, place = mesh_groups()
    groups = len(along[0])
    share = n_rel // groups

    def exchange(pieces, axis, index_groups):
        return lax.all_to_all(pieces, axis, 0, 0, axis_index_groups=index_groups)

    pieces = exchange(rel_grad.reshape(groups, share, width), ("dom", "bucket"), along)

    far_grad, grad_b = call(
        other_block,
        (mine, edge_count, edge_ends, far, q, scale, count, high, low),
        (shape((width, rows), BF16), shape(narrow, BF16)),
        "ssvhhhhhh",
        "vb",
        (
            pltpu.VMEM((width, rows), BF16),
            pltpu.VMEM(wide, BF16),
            pltpu.VMEM(narrow, F32),
            pltpu.VMEM((rows, 128), F32),
            pltpu.VMEM((rows, edges), BF16),
            pltpu.VMEM((rows, edges), BF16),
            pltpu.SemaphoreType.DMA((6,)),
        ),
    )
    home_grad = passed_along(far_grad, "dom", half_dom)

    first = place * share
    my_rel = lax.dynamic_slice_in_dim(relations, first, share, 0)
    my_state = lax.dynamic_slice_in_dim(relation_state, first, share, 0)[:, None]
    pieces, far_grad = lax.optimization_barrier((pieces, far_grad))
    stack = (shape((len(across[0]), share, width), F32),)
    (partial,) = call(sum_spread, (pieces,), stack, "v", "b")
    totals = exchange(partial, ("dom", "depth"), across)
    stack = (shape((groups, share, width), F32),)
    (new_rel,) = call(update_relations, (totals, my_rel, my_state), stack, "vvv", "b")
    new_relations = exchange(new_rel, ("dom", "bucket"), along).reshape(n_rel, width)

    new_state, new_entities = call(
        update_entities,
        (mine, edge_ends, entity_state.reshape(1, rows), home_grad, entities.T, grad_a, grad_b),
        (shape((1, rows), F32), shape((width, rows), F32)),
        "svvvhhh",
        "vh",
        (
            pltpu.VMEM((width, rows), F32),
            pltpu.VMEM(wide, BF16),
            pltpu.VMEM((width, rows), F32),
            pltpu.SemaphoreType.DMA((7,)),
        ),
    )
    return (new_entities.T, new_state.reshape(rows), new_relations)


def solution(mesh):
    return jax.shard_map(
        local,
        mesh=mesh,
        in_specs=(
            P(("dom", "bucket"), None),
            P(("dom", "bucket")),
            P(),
            P(),
            P(None, ("dom", "bucket")),
            P(("dom", "bucket")),
            P(("dom", "bucket"), "depth"),
            P(("dom", "bucket")),
        ),
        out_specs=(P(("dom", "bucket"), None), P(("dom", "bucket")), P()),
        check_vma=False,
    )
```

```python
import jax
import jax.numpy as jnp
from jax import lax
from jax.experimental import pallas as pl
from jax.experimental.pallas import tpu as pltpu
from jax.sharding import PartitionSpec as P

BLOCK = 512


entity_rate = 0.1
relation_rate = 1.0

F32 = jnp.float32
BF16 = jnp.bfloat16
NN = (((1,), (0,)), ((), ()))
NT = (((1,), (1,)), ((), ()))


def mm(a, b, dims=NN):
    return lax.dot_general(a, b, dims, preferred_element_type=F32)


def onehot(ids, rows):
    index = lax.broadcasted_iota(jnp.int32, (rows, ids.shape[1]), 0)
    return jnp.where(index == ids, 1.0, 0.0).astype(BF16)


def split(value, parts):
    out = []
    for _ in range(parts):
        piece = value.astype(BF16)
        out.append(piece)
        value = value - piece.astype(F32)
    return out


def pack(depth, ent_hbm, outer, middle, own, ent, sems):
    edge, half = outer.shape[1], middle.shape[1]
    rest = own.shape[1] - edge
    first = pl.ds(pl.multiple_of(depth[0] * rest, edge), edge)
    last = pl.ds(pl.multiple_of((1 - depth[0]) * rest, edge), edge)
    reads = [
        pltpu.make_async_copy(ent_hbm.at[:, lanes], ent.at[:, lanes], sems.at[i])
        for i, lanes in enumerate([first, pl.ds(edge, half), last])
    ]
    for read in reads:
        read.start()
    reads[0].wait()
    piece = ent[:, first].astype(BF16)
    outer[...] = piece
    own[:, first] = piece
    reads[1].wait()
    piece = ent[:, edge:rest].astype(BF16)
    middle[...] = piece
    own[:, edge:rest] = piece
    reads[2].wait()
    own[:, last] = ent[:, last].astype(BF16)


def prepare(own, ends, rid, neg_a, neg_b, rel_hbm, q, left, scale, count, rel, sems):
    read = pltpu.make_async_copy(rel_hbm, rel, sems.at[0])
    read.start()
    ones = jnp.ones((neg_a.shape[1], 128), BF16)
    blocks = q.shape[1] // BLOCK
    for c in range(blocks):
        hits = mm(onehot(neg_a[c : c + 1, :], own.shape[1]), ones)
        count[c] = hits + mm(onehot(neg_b[c : c + 1, :], own.shape[1]), ones)
    read.wait()
    rel_parts = split(rel[...], 3)
    for c in range(blocks):
        lanes = slice(c * BLOCK, (c + 1) * BLOCK)
        picked = mm(own[...], onehot(ends[0:1, lanes], own.shape[1]))
        by_rel = onehot(rid[0:1, lanes], rel.shape[1])
        factor = sum(mm(part, by_rel) for part in rel_parts)
        q[:, lanes] = (picked * factor).astype(BF16)
        left[:, lanes] = picked.astype(BF16)
        scale[:, lanes] = factor


CHUNK = 512
TILE = 256


def block_lanes(block):
    return pl.ds(pl.multiple_of(block * BLOCK, BLOCK), BLOCK)


def softmax_coef(scores, times, right_ids, first, live):
    right = lax.broadcasted_iota(jnp.int32, scores.shape, 0) == right_ids
    positive = jnp.sum(jnp.where(right, scores, 0.0), axis=0, keepdims=True)
    masked = jnp.where(times > 0.0, scores, -3.0e38)
    peak = jnp.maximum(positive, jnp.max(masked, axis=0, keepdims=True))
    shifted = jnp.exp(masked - peak)
    top = jnp.exp(positive - peak)
    denom = top + jnp.sum(shifted * times, axis=0, keepdims=True)
    slot = lax.broadcasted_iota(jnp.int32, right_ids.shape, 1) + first
    active = jnp.where(slot < live, 1.0, 0.0)
    pos_coef = active * (top / denom - 1.0)
    weights = (shifted * (active / denom)).astype(BF16).astype(F32) * times
    return split(weights + jnp.where(right, pos_coef, 0.0), 2)


def own_block(
    block, live, ends, rid, outer, middle, peer, q, left, scale, count,
    high_hbm, low_hbm, grad_hbm, rel_hbm, far_hbm,
    high, low, grad, rel_grad, far, sems,
):
    edge, rest = outer.shape[1], far.shape[1] - outer.shape[1]
    far[:, pl.ds(pl.multiple_of(block[0] * rest, edge), edge)] = outer[...]
    far[:, edge:rest] = middle[...]
    far[:, pl.ds(pl.multiple_of((1 - block[0]) * rest, edge), edge)] = peer[...]
    keep = pltpu.make_async_copy(far, far_hbm, sems.at[3 * (BLOCK // CHUNK) + 1])
    keep.start()
    far_rows = far[...].T
    times = jnp.tile(count[block[0]], (1, CHUNK // 128))
    total, writes = None, [keep]
    for c in range(BLOCK // CHUNK):
        part = slice(c * CHUNK, (c + 1) * CHUNK)
        first = pl.multiple_of(block[0] * BLOCK + c * CHUNK, CHUNK)
        ids = pl.ds(first, CHUNK)
        scores = mm(far_rows, q[:, ids])
        upper, lower = softmax_coef(scores, times, ends[1:2, ids], first, live[0])
        high[:, part] = upper
        low[:, part] = lower
        query_grad = mm(far[...], upper) + mm(far[...], lower)
        grad[:, part] = (query_grad * scale[:, ids]).astype(BF16)
        for i, (src, dst) in enumerate([(high, high_hbm), (low, low_hbm), (grad, grad_hbm)]):
            write = pltpu.make_async_copy(
                src.at[:, part], dst.at[:, part], sems.at[3 * c + i]
            )
            write.start()
            writes.append(write)
        pieces = split(query_grad * left[:, ids].astype(F32), 2)
        by_rel = onehot(rid[0:1, ids], rel_grad.shape[0])
        share = mm(by_rel, pieces[0], NT) + mm(by_rel, pieces[1], NT)
        total = share if total is None else total + share
    rel_grad[...] = total
    write = pltpu.make_async_copy(rel_grad, rel_hbm, sems.at[3 * (BLOCK // CHUNK)])
    write.start()
    writes.append(write)
    for write in writes:
        write.wait()


def dithered(value):
    row = lax.broadcasted_iota(jnp.int32, (value.shape[0], 1), 0).astype(F32) * 0.61803398875
    shift = (row - jnp.floor(row) - 0.5) * (1.0 / 256.0)
    return (value + value * shift).astype(BF16)


def other_block(
    block, live, ends, far_hbm, q_hbm, scale_hbm, count_hbm, high_hbm, low_hbm,
    far_grad, grad,
    far, q, scale, count, high, low, sems,
):
    lanes = block_lanes(1 - block[0])
    done = block_lanes(block[0])
    reads = [
        pltpu.make_async_copy(src, dst, sems.at[i])
        for i, (src, dst) in enumerate(
            [
                (far_hbm, far),
                (q_hbm, q),
                (count_hbm.at[1 - block[0]], count),
                (scale_hbm.at[:, lanes], scale),
                (high_hbm, high.at[:, done]),
                (low_hbm, low.at[:, done]),
            ]
        )
    ]
    for read in reads:
        read.start()
    for read in reads[:4]:
        read.wait()
    far_rows = far[...].T
    times = jnp.tile(count[...], (1, CHUNK // 128))
    for c in range(BLOCK // CHUNK):
        first = pl.multiple_of((1 - block[0]) * BLOCK + c * CHUNK, CHUNK)
        ids = pl.ds(first, CHUNK)
        scores = mm(far_rows, q[:, ids])
        upper, lower = softmax_coef(scores, times, ends[1:2, ids], first, live[0])
        high[:, ids] = upper
        low[:, ids] = lower
        query_grad = mm(far[...], upper) + mm(far[...], lower)
        part = slice(c * CHUNK, (c + 1) * CHUNK)
        grad[:, part] = (query_grad * scale[:, part]).astype(BF16)
    for read in reads[4:]:
        read.wait()
    for c in range(far_grad.shape[1] // TILE):
        part = slice(c * TILE, (c + 1) * TILE)
        both = mm(q[...], high[part, :], NT) + mm(q[...], low[part, :], NT)
        far_grad[:, part] = dithered(both)


def update_entities(
    block, ends, state, home, ent_hbm, grad_a, grad_b, new_state, new_hbm,
    ent, grad, new, sems,
):
    reads = [
        pltpu.make_async_copy(src, dst, sems.at[i])
        for i, (src, dst) in enumerate(
            [
                (grad_a, grad.at[:, block_lanes(block[0])]),
                (grad_b, grad.at[:, block_lanes(1 - block[0])]),
                (ent_hbm, ent),
            ]
        )
    ]
    for read in reads:
        read.start()
    for read in reads:
        read.wait()
    writes = []
    for c in range(ent.shape[1] // TILE):
        part = slice(c * TILE, (c + 1) * TILE)
        index = lax.broadcasted_iota(jnp.int32, (TILE, ends.shape[1]), 0) + c * TILE
        chosen = jnp.where(index == ends[0:1, :], 1.0, 0.0).astype(BF16)
        total = mm(grad[...], chosen, NT) + home[:, part].astype(F32)
        updated = state[0:1, part] + jnp.mean(total * total, axis=0, keepdims=True)
        new_state[0:1, part] = updated
        new[:, part] = ent[:, part] - entity_rate * total / jnp.sqrt(updated)
        write = pltpu.make_async_copy(new.at[:, part], new_hbm.at[:, part], sems.at[3 + c])
        write.start()
        writes.append(write)
    for write in writes:
        write.wait()


def sum_spread(pieces, out):
    out[...] = jnp.broadcast_to(jnp.sum(pieces[...], axis=0, keepdims=True), out.shape)


def update_relations(pieces, rel, state, out):
    total = jnp.sum(pieces[...], axis=0)
    updated = state[...] + jnp.mean(total * total, axis=1, keepdims=True)
    new = rel[...] - relation_rate * total / jnp.sqrt(updated)
    out[...] = jnp.broadcast_to(new[None], out.shape)


def call(kernel, args, outs, spaces, out_spaces, scratch=()):
    def spec(space, shape):
        if space == "b":
            return pl.BlockSpec(shape, lambda: (0,) * len(shape))
        return pl.BlockSpec(memory_space={"s": pltpu.SMEM, "v": pltpu.VMEM, "h": pltpu.HBM}[space])

    args = [
        pltpu.with_memory_space_constraint(arg, pltpu.HBM) if space in "hb" else arg
        for space, arg in zip(spaces, args, strict=True)
    ]
    return pl.pallas_call(
        kernel,
        out_shape=[
            pltpu.HBM(out.shape, out.dtype) if space in "hb" else out
            for space, out in zip(out_spaces, outs, strict=True)
        ],
        in_specs=[spec(space, arg.shape) for space, arg in zip(spaces, args, strict=True)],
        out_specs=[spec(space, out.shape) for space, out in zip(out_spaces, outs, strict=True)],
        scratch_shapes=list(scratch),
        compiler_params=pltpu.CompilerParams(vmem_limit_bytes=24 << 20),
    )(*args)


def passed_along(block, axis, distance):
    size = lax.axis_size(axis)
    return lax.ppermute(block, axis, [((i - distance) % size, i) for i in range(size)])


AXES = ("dom", "bucket", "depth")


def mesh_groups():
    n_z, n_k = lax.axis_size("bucket"), lax.axis_size("depth")
    n_x, n_y, n_core, near = 4, lax.axis_size("dom") // 8, 2, 2

    def device(x, y, core, high, low, k):
        return (((x * n_y + y) * n_core + core) * n_z + high * near + low) * n_k + k

    inside = [
        (x, core, low, k)
        for x in range(n_x)
        for core in range(n_core)
        for low in range(near)
        for k in range(n_k)
    ]
    outside = [(y, high) for y in range(n_y) for high in range(n_z // near)]
    along = [[device(x, y, c, high, low, k) for x, c, low, k in inside] for y, high in outside]
    across = [[device(x, y, c, high, low, k) for y, high in outside] for x, c, low, k in inside]
    dom = lax.axis_index("dom")
    place = dom // (n_y * n_core) * n_core + dom % n_core
    place = place * near + lax.axis_index("bucket") % near
    return along, across, place * n_k + lax.axis_index("depth")


def local(
    entities, entity_state, relations, relation_state, edge_ends, relation_ids, neg_ids, edge_count
):
    half_dom = lax.axis_size("dom") // 2
    rows, width = entities.shape
    n_rel = relations.shape[0]
    edges = relation_ids.shape[0]
    shape = jax.ShapeDtypeStruct
    rid = relation_ids.reshape(1, edges)

    neg_other = passed_along(neg_ids, "depth", 1)
    depth = lax.axis_index("depth").astype(jnp.int32)
    edge = rows // 4
    mine = depth.reshape(1)
    outer, middle, own = call(
        pack,
        (mine, entities.T),
        (shape((width, edge), BF16), shape((width, rows - 2 * edge), BF16), shape((width, rows), BF16)),
        "sh",
        "vvv",
        (pltpu.VMEM((width, rows), F32), pltpu.SemaphoreType.DMA((3,))),
    )
    outer = passed_along(outer, "dom", half_dom)
    middle = passed_along(middle, "dom", half_dom)
    peer = passed_along(outer, "depth", 1)
    own, outer = lax.optimization_barrier((own, outer))

    blocks = neg_ids.shape[0]
    wide, narrow = (width, edges), (width, BLOCK)
    q, left, scale, count = call(
        prepare,
        (own, edge_ends, rid, neg_ids, neg_other, relations.T),
        (shape(wide, BF16), shape(wide, BF16), shape(wide, F32), shape((blocks, rows, 128), F32)),
        "vvvvvh",
        "vvvv",
        (pltpu.VMEM((width, n_rel), F32), pltpu.SemaphoreType.DMA((1,))),
    )
    mat = (rows, BLOCK)
    high, low, grad_a, rel_grad, far = call(
        own_block,
        (mine, edge_count, edge_ends, rid, outer, middle, peer, q, left, scale, count),
        (
            shape(mat, BF16),
            shape(mat, BF16),
            shape(narrow, BF16),
            shape((n_rel, width), F32),
            shape((width, rows), BF16),
        ),
        "ssvvvvvvvvv",
        "hhhhh",
        (
            pltpu.VMEM(mat, BF16),
            pltpu.VMEM(mat, BF16),
            pltpu.VMEM(narrow, BF16),
            pltpu.VMEM((n_rel, width), F32),
            pltpu.VMEM((width, rows), BF16),
            pltpu.SemaphoreType.DMA((3 * (BLOCK // CHUNK) + 2,)),
        ),
    )
    along, across, place = mesh_groups()
    groups = len(along[0])
    share = n_rel // groups

    def exchange(pieces, index_groups):
        return lax.all_to_all(pieces, AXES, 0, 0, axis_index_groups=index_groups)

    pieces = exchange(rel_grad.reshape(groups, share, width), along)

    far_grad, grad_b = call(
        other_block,
        (mine, edge_count, edge_ends, far, q, scale, count, high, low),
        (shape((width, rows), BF16), shape(narrow, BF16)),
        "ssvhhhhhh",
        "vb",
        (
            pltpu.VMEM((width, rows), BF16),
            pltpu.VMEM(wide, BF16),
            pltpu.VMEM(narrow, F32),
            pltpu.VMEM((rows, 128), F32),
            pltpu.VMEM((rows, edges), BF16),
            pltpu.VMEM((rows, edges), BF16),
            pltpu.SemaphoreType.DMA((6,)),
        ),
    )
    home_grad = passed_along(far_grad, "dom", half_dom)

    first = place * share
    my_rel = lax.dynamic_slice_in_dim(relations, first, share, 0)
    my_state = lax.dynamic_slice_in_dim(relation_state, first, share, 0)[:, None]
    pieces, far_grad = lax.optimization_barrier((pieces, far_grad))
    stack = (shape((len(across[0]), share, width), F32),)
    (partial,) = call(sum_spread, (pieces,), stack, "v", "b")
    totals = exchange(partial, across)
    stack = (shape((groups, share, width), F32),)
    (new_rel,) = call(update_relations, (totals, my_rel, my_state), stack, "vvv", "b")
    new_relations = exchange(new_rel, along).reshape(n_rel, width)

    new_state, new_entities = call(
        update_entities,
        (mine, edge_ends, entity_state.reshape(1, rows), home_grad, entities.T, grad_a, grad_b),
        (shape((1, rows), F32), shape((width, rows), F32)),
        "svvvhhh",
        "vh",
        (
            pltpu.VMEM((width, rows), F32),
            pltpu.VMEM(wide, BF16),
            pltpu.VMEM((width, rows), F32),
            pltpu.SemaphoreType.DMA((7,)),
        ),
    )
    return (new_entities.T, new_state.reshape(rows), new_relations)


def solution(mesh):
    return jax.shard_map(
        local,
        mesh=mesh,
        in_specs=(
            P(("dom", "bucket"), None),
            P(("dom", "bucket")),
            P(),
            P(),
            P(None, ("dom", "bucket")),
            P(("dom", "bucket")),
            P(("dom", "bucket"), "depth"),
            P(("dom", "bucket")),
        ),
        out_specs=(P(("dom", "bucket"), None), P(("dom", "bucket")), P()),
        check_vma=False,
    )
```

```python
import jax
import jax.numpy as jnp
from jax import lax
from jax.experimental import pallas as pl
from jax.experimental.pallas import tpu as pltpu
from jax.sharding import PartitionSpec as P

BLOCK = 512


entity_rate = 0.1
relation_rate = 1.0

F32 = jnp.float32
BF16 = jnp.bfloat16
NN = (((1,), (0,)), ((), ()))
NT = (((1,), (1,)), ((), ()))


def mm(a, b, dims=NN):
    return lax.dot_general(a, b, dims, preferred_element_type=F32)


def onehot(ids, rows):
    index = lax.broadcasted_iota(jnp.int32, (rows, ids.shape[1]), 0)
    return jnp.where(index == ids, 1.0, 0.0).astype(BF16)


def split(value, parts):
    out = []
    for _ in range(parts):
        piece = value.astype(BF16)
        out.append(piece)
        value = value - piece.astype(F32)
    return out


def pack(depth, ent_hbm, outer, middle, own, ent, sems):
    edge, half = outer.shape[1], middle.shape[1]
    rest = own.shape[1] - edge
    first = pl.ds(pl.multiple_of(depth[0] * rest, edge), edge)
    last = pl.ds(pl.multiple_of((1 - depth[0]) * rest, edge), edge)
    reads = [
        pltpu.make_async_copy(ent_hbm.at[:, lanes], ent.at[:, lanes], sems.at[i])
        for i, lanes in enumerate([first, pl.ds(edge, half), last])
    ]
    for read in reads:
        read.start()
    reads[0].wait()
    piece = ent[:, first].astype(BF16)
    outer[...] = piece
    own[:, first] = piece
    reads[1].wait()
    piece = ent[:, edge:rest].astype(BF16)
    middle[...] = piece
    own[:, edge:rest] = piece
    reads[2].wait()
    own[:, last] = ent[:, last].astype(BF16)


def prepare(own, ends, rid, neg_a, neg_b, rel_hbm, q, left, scale, count, rel, sems):
    read = pltpu.make_async_copy(rel_hbm, rel, sems.at[0])
    read.start()
    ones = jnp.ones((neg_a.shape[1], 128), BF16)
    blocks = q.shape[1] // BLOCK
    for c in range(blocks):
        hits = mm(onehot(neg_a[c : c + 1, :], own.shape[1]), ones)
        count[c] = hits + mm(onehot(neg_b[c : c + 1, :], own.shape[1]), ones)
    read.wait()
    rel_parts = split(rel[...], 3)
    for c in range(blocks):
        lanes = slice(c * BLOCK, (c + 1) * BLOCK)
        picked = mm(own[...], onehot(ends[0:1, lanes], own.shape[1]))
        by_rel = onehot(rid[0:1, lanes], rel.shape[1])
        factor = sum(mm(part, by_rel) for part in rel_parts)
        q[:, lanes] = (picked * factor).astype(BF16)
        left[:, lanes] = picked.astype(BF16)
        scale[:, lanes] = factor


CHUNK = 512
TILE = 256


def block_lanes(block):
    return pl.ds(pl.multiple_of(block * BLOCK, BLOCK), BLOCK)


def softmax_coef(scores, times, right_ids, first, live):
    right = lax.broadcasted_iota(jnp.int32, scores.shape, 0) == right_ids
    positive = jnp.sum(jnp.where(right, scores, 0.0), axis=0, keepdims=True)
    masked = jnp.where(times > 0.0, scores, -3.0e38)
    peak = jnp.maximum(positive, jnp.max(masked, axis=0, keepdims=True))
    shifted = jnp.exp(masked - peak)
    top = jnp.exp(positive - peak)
    denom = top + jnp.sum(shifted * times, axis=0, keepdims=True)
    slot = lax.broadcasted_iota(jnp.int32, right_ids.shape, 1) + first
    active = jnp.where(slot < live, 1.0, 0.0)
    pos_coef = active * (top / denom - 1.0)
    weights = (shifted * (active / denom)).astype(BF16).astype(F32) * times
    return split(weights + jnp.where(right, pos_coef, 0.0), 2)


def own_block(
    block, live, ends, rid, outer, middle, peer, q, left, scale, count,
    high_hbm, low_hbm, grad_hbm, rel_hbm, far_hbm,
    high, low, grad, rel_grad, far, sems,
):
    edge, rest = outer.shape[1], far.shape[1] - outer.shape[1]
    far[:, pl.ds(pl.multiple_of(block[0] * rest, edge), edge)] = outer[...]
    far[:, edge:rest] = middle[...]
    far[:, pl.ds(pl.multiple_of((1 - block[0]) * rest, edge), edge)] = peer[...]
    keep = pltpu.make_async_copy(far, far_hbm, sems.at[3 * (BLOCK // CHUNK) + 1])
    keep.start()
    far_rows = far[...].T
    times = jnp.tile(count[block[0]], (1, CHUNK // 128))
    total, writes = None, [keep]
    for c in range(BLOCK // CHUNK):
        part = slice(c * CHUNK, (c + 1) * CHUNK)
        first = pl.multiple_of(block[0] * BLOCK + c * CHUNK, CHUNK)
        ids = pl.ds(first, CHUNK)
        scores = mm(far_rows, q[:, ids])
        upper, lower = softmax_coef(scores, times, ends[1:2, ids], first, live[0])
        high[:, part] = upper
        low[:, part] = lower
        query_grad = mm(far[...], upper) + mm(far[...], lower)
        grad[:, part] = (query_grad * scale[:, ids]).astype(BF16)
        for i, (src, dst) in enumerate([(high, high_hbm), (low, low_hbm), (grad, grad_hbm)]):
            write = pltpu.make_async_copy(
                src.at[:, part], dst.at[:, part], sems.at[3 * c + i]
            )
            write.start()
            writes.append(write)
        pieces = split(query_grad * left[:, ids].astype(F32), 2)
        by_rel = onehot(rid[0:1, ids], rel_grad.shape[0])
        share = mm(by_rel, pieces[0], NT) + mm(by_rel, pieces[1], NT)
        total = share if total is None else total + share
    rel_grad[...] = total
    write = pltpu.make_async_copy(rel_grad, rel_hbm, sems.at[3 * (BLOCK // CHUNK)])
    write.start()
    writes.append(write)
    for write in writes:
        write.wait()


def dithered(value):
    row = lax.broadcasted_iota(jnp.int32, (value.shape[0], 1), 0).astype(F32) * 0.61803398875
    shift = (row - jnp.floor(row) - 0.5) * (1.0 / 256.0)
    return (value + value * shift).astype(BF16)


def other_block(
    block, live, ends, far_hbm, q_hbm, count_hbm, high_hbm, low_hbm,
    far_grad, high_out, low_out,
    far, q, count, high, low, sems,
):
    done = block_lanes(block[0])
    lanes = block_lanes(1 - block[0])
    reads = [
        pltpu.make_async_copy(src, dst, sems.at[i])
        for i, (src, dst) in enumerate(
            [
                (far_hbm, far),
                (q_hbm, q),
                (count_hbm.at[1 - block[0]], count),
                (high_hbm, high.at[:, done]),
                (low_hbm, low.at[:, done]),
            ]
        )
    ]
    for read in reads:
        read.start()
    for read in reads[:3]:
        read.wait()
    scores = mm(far[...].T, q[:, lanes])
    times = jnp.tile(count[...], (1, BLOCK // 128))
    first = (1 - block[0]) * BLOCK
    upper, lower = softmax_coef(scores, times, ends[1:2, lanes], first, live[0])
    high[:, lanes] = upper
    low[:, lanes] = lower
    writes = [
        pltpu.make_async_copy(high.at[:, lanes], high_out, sems.at[5]),
        pltpu.make_async_copy(low.at[:, lanes], low_out, sems.at[6]),
    ]
    for write in writes:
        write.start()
    for read in reads[3:]:
        read.wait()
    for c in range(far_grad.shape[1] // TILE):
        part = slice(c * TILE, (c + 1) * TILE)
        both = mm(q[...], high[part, :], NT) + mm(q[...], low[part, :], NT)
        far_grad[:, part] = dithered(both)
    for write in writes:
        write.wait()


def own_side(
    block, ends, far_hbm, high_hbm, low_hbm, scale_hbm, grad_hbm, own_hbm,
    far, high, low, scale, grad, own, sems,
):
    lanes = block_lanes(1 - block[0])
    reads = [
        pltpu.make_async_copy(src, dst, sems.at[i])
        for i, (src, dst) in enumerate(
            [
                (far_hbm, far),
                (high_hbm, high),
                (low_hbm, low),
                (scale_hbm.at[:, lanes], scale),
                (grad_hbm, grad.at[:, block_lanes(block[0])]),
            ]
        )
    ]
    for read in reads:
        read.start()
    for read in reads:
        read.wait()
    query_grad = mm(far[...], high[...]) + mm(far[...], low[...])
    grad[:, lanes] = (query_grad * scale[...]).astype(BF16)
    writes = []
    for c in range(own.shape[1] // TILE):
        part = slice(c * TILE, (c + 1) * TILE)
        index = lax.broadcasted_iota(jnp.int32, (TILE, ends.shape[1]), 0) + c * TILE
        chosen = jnp.where(index == ends[0:1, :], 1.0, 0.0).astype(BF16)
        own[:, part] = mm(grad[...], chosen, NT)
        write = pltpu.make_async_copy(own.at[:, part], own_hbm.at[:, part], sems.at[5 + c])
        write.start()
        writes.append(write)
    for write in writes:
        write.wait()


def update_entities(state, home, own_hbm, ent_hbm, new_state, new_hbm, own, ent, new, sems):
    parts = [slice(c * TILE, (c + 1) * TILE) for c in range(ent.shape[1] // TILE)]
    reads = [
        (
            pltpu.make_async_copy(own_hbm.at[:, part], own.at[:, part], sems.at[3 * c]),
            pltpu.make_async_copy(ent_hbm.at[:, part], ent.at[:, part], sems.at[3 * c + 1]),
        )
        for c, part in enumerate(parts)
    ]
    for pair in reads:
        for read in pair:
            read.start()
    writes = []
    for c, part in enumerate(parts):
        for read in reads[c]:
            read.wait()
        total = own[:, part] + home[:, part].astype(F32)
        updated = state[0:1, part] + jnp.mean(total * total, axis=0, keepdims=True)
        new_state[0:1, part] = updated
        new[:, part] = ent[:, part] - entity_rate * total / jnp.sqrt(updated)
        write = pltpu.make_async_copy(new.at[:, part], new_hbm.at[:, part], sems.at[3 * c + 2])
        write.start()
        writes.append(write)
    for write in writes:
        write.wait()


def sum_spread(pieces, out):
    out[...] = jnp.broadcast_to(jnp.sum(pieces[...], axis=0, keepdims=True), out.shape)


def update_relations(pieces, rel, state, out):
    total = jnp.sum(pieces[...], axis=0)
    updated = state[...] + jnp.mean(total * total, axis=1, keepdims=True)
    new = rel[...] - relation_rate * total / jnp.sqrt(updated)
    out[...] = jnp.broadcast_to(new[None], out.shape)


def call(kernel, args, outs, spaces, out_spaces, scratch=()):
    def spec(space, shape):
        if space == "b":
            return pl.BlockSpec(shape, lambda: (0,) * len(shape))
        return pl.BlockSpec(memory_space={"s": pltpu.SMEM, "v": pltpu.VMEM, "h": pltpu.HBM}[space])

    args = [
        pltpu.with_memory_space_constraint(arg, pltpu.HBM) if space in "hb" else arg
        for space, arg in zip(spaces, args, strict=True)
    ]
    return pl.pallas_call(
        kernel,
        out_shape=[
            pltpu.HBM(out.shape, out.dtype) if space in "hb" else out
            for space, out in zip(out_spaces, outs, strict=True)
        ],
        in_specs=[spec(space, arg.shape) for space, arg in zip(spaces, args, strict=True)],
        out_specs=[spec(space, out.shape) for space, out in zip(out_spaces, outs, strict=True)],
        scratch_shapes=list(scratch),
        compiler_params=pltpu.CompilerParams(vmem_limit_bytes=24 << 20),
    )(*args)


def passed_along(block, axis, distance):
    size = lax.axis_size(axis)
    return lax.ppermute(block, axis, [((i - distance) % size, i) for i in range(size)])


AXES = ("dom", "bucket", "depth")


def mesh_groups():
    n_z, n_k = lax.axis_size("bucket"), lax.axis_size("depth")
    n_x, n_y, n_core, near = 4, lax.axis_size("dom") // 8, 2, 2

    def device(x, y, core, high, low, k):
        return (((x * n_y + y) * n_core + core) * n_z + high * near + low) * n_k + k

    inside = [
        (x, core, low, k)
        for x in range(n_x)
        for core in range(n_core)
        for low in range(near)
        for k in range(n_k)
    ]
    outside = [(y, high) for y in range(n_y) for high in range(n_z // near)]
    along = [[device(x, y, c, high, low, k) for x, c, low, k in inside] for y, high in outside]
    across = [[device(x, y, c, high, low, k) for y, high in outside] for x, c, low, k in inside]
    dom = lax.axis_index("dom")
    place = dom // (n_y * n_core) * n_core + dom % n_core
    place = place * near + lax.axis_index("bucket") % near
    return along, across, place * n_k + lax.axis_index("depth")


def local(
    entities, entity_state, relations, relation_state, edge_ends, relation_ids, neg_ids, edge_count
):
    half_dom = lax.axis_size("dom") // 2
    rows, width = entities.shape
    n_rel = relations.shape[0]
    edges = relation_ids.shape[0]
    shape = jax.ShapeDtypeStruct
    rid = relation_ids.reshape(1, edges)

    neg_other = passed_along(neg_ids, "depth", 1)
    depth = lax.axis_index("depth").astype(jnp.int32)
    edge = rows // 4
    mine = depth.reshape(1)
    outer, middle, own = call(
        pack,
        (mine, entities.T),
        (shape((width, edge), BF16), shape((width, rows - 2 * edge), BF16), shape((width, rows), BF16)),
        "sh",
        "vvv",
        (pltpu.VMEM((width, rows), F32), pltpu.SemaphoreType.DMA((3,))),
    )
    outer = passed_along(outer, "dom", half_dom)
    middle = passed_along(middle, "dom", half_dom)
    peer = passed_along(outer, "depth", 1)
    own, outer = lax.optimization_barrier((own, outer))

    blocks = neg_ids.shape[0]
    wide, narrow = (width, edges), (width, BLOCK)
    q, left, scale, count = call(
        prepare,
        (own, edge_ends, rid, neg_ids, neg_other, relations.T),
        (shape(wide, BF16), shape(wide, BF16), shape(wide, F32), shape((blocks, rows, 128), F32)),
        "vvvvvh",
        "vvvv",
        (pltpu.VMEM((width, n_rel), F32), pltpu.SemaphoreType.DMA((1,))),
    )
    mat = (rows, BLOCK)
    high, low, grad_a, rel_grad, far = call(
        own_block,
        (mine, edge_count, edge_ends, rid, outer, middle, peer, q, left, scale, count),
        (
            shape(mat, BF16),
            shape(mat, BF16),
            shape(narrow, BF16),
            shape((n_rel, width), F32),
            shape((width, rows), BF16),
        ),
        "ssvvvvvvvvv",
        "hhhhh",
        (
            pltpu.VMEM(mat, BF16),
            pltpu.VMEM(mat, BF16),
            pltpu.VMEM(narrow, BF16),
            pltpu.VMEM((n_rel, width), F32),
            pltpu.VMEM((width, rows), BF16),
            pltpu.SemaphoreType.DMA((3 * (BLOCK // CHUNK) + 2,)),
        ),
    )
    along, across, place = mesh_groups()
    groups = len(along[0])
    share = n_rel // groups

    def exchange(pieces, index_groups):
        return lax.all_to_all(pieces, AXES, 0, 0, axis_index_groups=index_groups)

    pieces = exchange(rel_grad.reshape(groups, share, width), along)

    far_grad, high_b, low_b = call(
        other_block,
        (mine, edge_count, edge_ends, far, q, count, high, low),
        (shape((width, rows), BF16), shape(mat, BF16), shape(mat, BF16)),
        "ssvhhhhh",
        "vhh",
        (
            pltpu.VMEM((width, rows), BF16),
            pltpu.VMEM(wide, BF16),
            pltpu.VMEM((rows, 128), F32),
            pltpu.VMEM((rows, edges), BF16),
            pltpu.VMEM((rows, edges), BF16),
            pltpu.SemaphoreType.DMA((7,)),
        ),
    )
    home_grad = passed_along(far_grad, "dom", half_dom)

    first = place * share
    my_rel = lax.dynamic_slice_in_dim(relations, first, share, 0)
    my_state = lax.dynamic_slice_in_dim(relation_state, first, share, 0)[:, None]
    pieces, far_grad = lax.optimization_barrier((pieces, far_grad))
    stack = (shape((len(across[0]), share, width), F32),)
    (partial,) = call(sum_spread, (pieces,), stack, "v", "b")
    totals = exchange(partial, across)
    stack = (shape((groups, share, width), F32),)
    (new_rel,) = call(update_relations, (totals, my_rel, my_state), stack, "vvv", "b")
    new_relations = exchange(new_rel, along).reshape(n_rel, width)

    (own_grad,) = call(
        own_side,
        (mine, edge_ends, far, high_b, low_b, scale, grad_a),
        (shape((width, rows), F32),),
        "svhhhhh",
        "h",
        (
            pltpu.VMEM((width, rows), BF16),
            pltpu.VMEM(mat, BF16),
            pltpu.VMEM(mat, BF16),
            pltpu.VMEM(narrow, F32),
            pltpu.VMEM(wide, BF16),
            pltpu.VMEM((width, rows), F32),
            pltpu.SemaphoreType.DMA((5 + rows // TILE,)),
        ),
    )
    new_state, new_entities = call(
        update_entities,
        (entity_state.reshape(1, rows), home_grad, own_grad, entities.T),
        (shape((1, rows), F32), shape((width, rows), F32)),
        "vvhh",
        "vh",
        (
            pltpu.VMEM((width, rows), F32),
            pltpu.VMEM((width, rows), F32),
            pltpu.VMEM((width, rows), F32),
            pltpu.SemaphoreType.DMA((3 * (rows // TILE),)),
        ),
    )
    return (new_entities.T, new_state.reshape(rows), new_relations)


def solution(mesh):
    return jax.shard_map(
        local,
        mesh=mesh,
        in_specs=(
            P(("dom", "bucket"), None),
            P(("dom", "bucket")),
            P(),
            P(),
            P(None, ("dom", "bucket")),
            P(("dom", "bucket")),
            P(("dom", "bucket"), "depth"),
            P(("dom", "bucket")),
        ),
        out_specs=(P(("dom", "bucket"), None), P(("dom", "bucket")), P()),
        check_vma=False,
    )
```
